512 devices in a mesh: dp: 16 (over z_hi, y), expert: 32 (over z_lo, x, core).
Axes of the slice: x: 4, y: 4, z: 16 (z_hi: 4, z_lo: 4; z = z_hi * 4 + z_lo), core: 2. Of those that a mesh axis runs over, the one named last changes fastest.
Arguments:
- tokens: bfloat16 [57344, 1024], P(('dp', 'expert')), parts along dimension 0, may hold values from -6 to 6
- expert_ids: int32 [57344, 8], P(('dp', 'expert')), parts along dimension 0, may hold values from 0 to 31, all different within a row; in each aligned block of 112 rows (0 to 111, 112 to 223, ...) at most 56 rows name the same one
- gate_probs: float32 [57344, 8], P(('dp', 'expert')), parts along dimension 0, may hold values from 0.05 to 0.5
- w_gate: bfloat16 [32, 1024, 384], P('expert'), may hold values from -0.1875 to 0.1875
- w_up: bfloat16 [32, 1024, 384], P('expert'), may hold values from -0.1875 to 0.1875
- w_down: bfloat16 [32, 384, 1024], P('expert'), may hold values from -0.3125 to 0.3125
- placement: int32 [32], replicated, may hold values from 0 to 31, each once
- swap_flags: int32 [32], replicated, may hold values from 0 to 1, as said below
Outputs:
- mixed: bfloat16 [57344, 1024], P(('dp', 'expert')), parts along dimension 0
- stored_gate: bfloat16 [512, 1024, 384], P(('dp', 'expert')), parts along dimension 0
- stored_up: bfloat16 [512, 1024, 384], P(('dp', 'expert')), parts along dimension 0
- stored_down: bfloat16 [512, 384, 1024], P(('dp', 'expert')), parts along dimension 0
The draws below stay inside these ranges and needn't reach their ends.
There are 16 independent parts, one for each index of `dp`. The reference program is written for one: setup_inputs(seed, part) draws one part's arguments, and reference() takes and returns one part's arrays. A program takes and returns all parts, laid end to end along the dimension named above; an argument that names none is the same for every part. Nothing has to cross between parts.
Inputs may be any that keep to these rules, and one draw needn't show every extreme that they name: `expert_ids`: each row names 8 different experts; the 112 rows of one device name one expert at most 56 times, a bound that some block reaches. `placement`: each expert is stored on exactly one device. swap_flags[d] equals swap_flags[d XOR (16)]; the number of devices is a power of two. The first and last pairs always trade, the second pair never does.
All inputs are finite; a program needn't handle non-finite values.
Results may differ from the reference program's by a relative error of at most 0.0057.
Values may be sent and summed in bfloat16 or wider, within the bound.
A program may use at most 64 MiB of HBM per device.

```python
import math
import jax
import jax.numpy as jnp
import numpy as np
from jax import lax

D = 1024
FF = 384
TOP = 8
TOK_DEV = 112
EXPERTS = 32
CAP = 56
TOKENS = 3584


def draw_swap_flags(key, part):
    halves = jax.random.randint(jax.random.fold_in(key, 7), (EXPERTS // 2,), 0, 2).astype(jnp.int32)
    halves = halves.at[0].set(1).at[1].set(0).at[EXPERTS // 2 - 1].set(1)
    return jnp.concatenate([halves, halves], axis=0)


def block_scale(key, dims, shards, low, high):
    factor_of = 1.0
    for dim, shards_of in shards:
        steps = jax.random.uniform(jax.random.fold_in(jax.random.fold_in(key, 6), dim), (shards_of,), jnp.float32, low / len(shards), high / len(shards))
        factor_of = factor_of * jnp.repeat(jnp.exp(steps), dims[dim] // shards_of).reshape((-1,) + (1,) * (len(dims) - 1 - dim))
    return factor_of


def routed_block(key, own, number, rows, count, top, bound, lean):
    sequence = jax.random.permutation(key, count)
    crowded, ordinary = shares(count, rows * top, bound, lean, True), shares(count, rows * top, bound, lean, False)
    places = jnp.arange(count)

    def named(tallies, rotation):
        used = int((tallies > 0).sum())
        fixed = max(1, used // 4)
        shifted = fixed + (places - fixed + rotation * (used - fixed)) % max(1, count - fixed)
        return jnp.zeros((count,), jnp.int32).at[sequence[jnp.where(places < fixed, places, shifted)]].set(jnp.asarray(tallies, jnp.int32))

    tallies = jnp.where(number % 4 == 0, named(crowded, number // 4), named(ordinary, number - number // 4 - 1))
    mixed = jax.random.permutation(jax.random.fold_in(own, 3), count)
    source_of, taker = mixed[0:count // 2 * 2:2], mixed[1:count // 2 * 2:2]
    room = jnp.minimum(tallies[source_of] - 1, bound - tallies[taker]) // 2
    room = jnp.where((source_of == sequence[0]) | (taker == sequence[0]) | (tallies[taker] == 0), 0, jnp.maximum(room, 0))
    shifted = jax.random.randint(jax.random.fold_in(own, 4), (count // 2,), 0, 1 << 20) % (room + 1)
    tallies = tallies.at[source_of].add(-shifted).at[taker].add(shifted)
    members = jnp.searchsorted(jnp.cumsum(tallies), jnp.arange(rows * top), side="right").astype(jnp.int32)
    listing = members.reshape(top, rows).T
    listing = listing[jax.random.permutation(jax.random.fold_in(own, 1), rows)]
    rotation = jax.random.randint(jax.random.fold_in(own, 2), (rows, 1), 0, top)
    return jnp.take_along_axis(listing, (jnp.arange(top)[None, :] + rotation) % top, axis=1)


def shares(amount, total, reach, slope, full):
    loads = [(1 << 20) // math.isqrt(standing ** slope) + 1 for standing in range(1, amount + 1)]
    largest = reach if full else min(reach, max(-(-total // amount), total * loads[0] // sum(loads)))
    least = 1 if total - largest >= amount - 1 else 0
    holding, surplus = [largest] + [least] * (amount - 1), total - largest - least * (amount - 1)
    while surplus > 0:
        candidates = [i for i in range(1, amount) if holding[i] < largest] or [i for i in range(1, amount) if holding[i] < reach]
        mass, remaining = sum([loads[i] for i in candidates]), surplus
        for i in candidates:
            addition = min(reach - holding[i], max(1, remaining * loads[i] // mass), surplus)
            holding[i] = holding[i] + addition
            surplus = surplus - addition
    return np.array(holding)


def centred(own_key, extent, width, limit, cuts=(), kind=jnp.bfloat16):
    entries = jax.random.normal(own_key, extent, jnp.float32) * width
    if len(cuts) > 0:
        entries = block_scale(own_key, extent, cuts, -0.22, 0.18) * entries
    return jnp.clip(entries, min=-limit, max=limit).astype(kind)


def setup_inputs(seed: int = 0, part: int = 0) -> dict:
    key_list = jax.random.split(jax.random.key(seed), 9)
    part_keys = jax.random.split(jax.random.fold_in(key_list[8], part), 9)
    tokens = centred(part_keys[0], (TOKENS, D), 1.0, 6.0, ((0, 32),))
    expert_ids_keys = jax.random.split(jax.random.fold_in(part_keys[1], 1), TOKENS // TOK_DEV)
    expert_ids_turns = jax.random.permutation(jax.random.fold_in(part_keys[1], 3), TOKENS // TOK_DEV)
    expert_ids = jax.vmap(lambda own, number: routed_block(jax.random.fold_in(part_keys[1], 2), own, number, TOK_DEV, EXPERTS, TOP, CAP, 2))(expert_ids_keys, expert_ids_turns).reshape((TOKENS, TOP))
    gate_probs = jnp.clip(jnp.exp(math.log(0.5) - 2.3025851 * jax.random.uniform(part_keys[2], (TOKENS, TOP), jnp.float32) ** block_scale(part_keys[2], (TOKENS, TOP), ((0, 32),), -0.2, 0.2)), 0.05, 0.5)
    w_gate = centred(key_list[3], (EXPERTS, D, FF), D ** -0.5, 0.1875, ((0, 32),))
    w_up = centred(key_list[4], (EXPERTS, D, FF), D ** -0.5, 0.1875, ((0, 32),))
    w_down = centred(key_list[5], (EXPERTS, FF, D), FF ** -0.5, 0.3125, ((0, 32),))
    placement = jax.random.permutation(key_list[6], EXPERTS).astype(jnp.int32)
    swap_flags = draw_swap_flags(jax.random.fold_in(key_list[8], 71), part)
    return dict(tokens=tokens, expert_ids=expert_ids, gate_probs=gate_probs, w_gate=w_gate, w_up=w_up, w_down=w_down, placement=placement, swap_flags=swap_flags)


def expert_apply(rows, gate_w, up_w, down_w):
    gate = jnp.dot(rows, gate_w, preferred_element_type=jnp.float32)
    upward = jnp.dot(rows, up_w, preferred_element_type=jnp.float32)
    hidden = (jax.nn.silu(gate) * upward).astype(jnp.bfloat16)
    return jnp.dot(hidden, down_w, preferred_element_type=jnp.float32).astype(jnp.bfloat16)


def reference(tokens, expert_ids, gate_probs, w_gate, w_up, w_down, placement, swap_flags):
    most_rows = EXPERTS * CAP

    def one_store(carry, stored):
        gate_w, up_w, down_w, expert = stored
        chosen = expert_ids == expert
        picked = jnp.any(chosen, axis=1)
        weight_row = jnp.sum(jnp.where(chosen, gate_probs, jnp.zeros_like(gate_probs)), axis=1)
        count = jnp.sum(picked.astype(jnp.int32))
        (row_index,) = jnp.nonzero(picked, size=most_rows, fill_value=0)
        row_index = row_index.astype(jnp.int32)
        live = jnp.arange(most_rows, dtype=jnp.int32) < count
        outputs = expert_apply(tokens[row_index], gate_w, up_w, down_w)
        outputs = jnp.where(live[:, None], outputs, jnp.zeros_like(outputs))
        values = outputs.astype(jnp.float32)
        carry = carry.at[row_index].add(weight_row[row_index][:, None] * values)
        return carry, None

    mixed, unused = lax.scan(one_store, jnp.zeros((TOKENS, D), jnp.float32), (w_gate, w_up, w_down, placement))
    devices = jnp.arange(EXPERTS, dtype=jnp.int32)
    partners = (devices + EXPERTS // 2) % EXPERTS
    source = jnp.where(swap_flags == 1, partners, devices).astype(jnp.int32)
    return mixed.astype(jnp.bfloat16), w_gate[source], w_up[source], w_down[source]
```

```python
import jax
import jax.numpy as jnp
from jax import lax
from jax.experimental import pallas as pl
from jax.experimental.pallas import tpu as pltpu
from jax.sharding import PartitionSpec as P

MESH = pl.DeviceIdType.MESH
F32 = jnp.float32
BF16 = jnp.bfloat16


class Links:
    def __init__(self, send, recv):
        self.send, self.recv, self.count, self.started = send, recv, 0, []

    def new(self):
        self.count += 1
        return self.count - 1

    def copy(self, k, src, dst, dev):
        return pltpu.make_async_remote_copy(
            src_ref=src,
            dst_ref=dst,
            send_sem=self.send.at[k],
            recv_sem=self.recv.at[k],
            device_id=dev,
            device_id_type=MESH,
        )

    def start(self, k, src, dst, dev):
        c = self.copy(k, src, dst, dev)
        c.start()
        self.started.append(c)

    def arrived(self, k, dst, dev):
        self.copy(k, dst, dst, dev).wait_recv()

    def finish(self):
        for c in self.started:
            c.wait_send()


def kernel(
    tok_ref, table_ref, flag_ref, wg_hbm, wu_hbm, wd_hbm,
    mixed_ref, sg_hbm, su_hbm, sd_hbm,
    x_buf, meta, gcol, wgu, wdn, hid, acc, sendb, half_in, full_in, z_in,
    sel_g, sel_u, sel_d, send_sem, recv_sem, local_sem,
):
    rows, width = tok_ref.shape
    ff = wg_hbm.shape[1]
    half = width // 2
    dp = lax.axis_index("dp")
    ex = lax.axis_index("expert")
    zh, y = dp // 4, dp % 4
    zl, x, c = ex // 8, (ex // 2) % 4, ex % 2
    zo = zl + 1 - 2 * (zl % 2)

    def at(dx, other):
        return {"dp": dp, "expert": ((zo if other else zl) * 4 + (x + dx + 4) % 4) * 2 + c}

    def at_z(d):
        zz = (zh * 4 + zl + d + 16) % 16
        return {"dp": (zz // 4) * 4 + y, "expert": ((zz % 4) * 4 + x) * 2 + c}

    def at_y(d):
        return {"dp": zh * 4 + (y + d + 4) % 4, "expert": ex}

    sibling = {"dp": dp, "expert": ex + 1 - 2 * c}
    xr, xl, zp = at(1, False), at(-1, False), at(0, True)
    peers = [at(1, False), at(-1, False), at(2, False), at(0, True), at(1, True), at(-1, True), at(2, True)]
    partners = peers + [at_z(2), at_z(-2), at_y(1), at_y(-1), sibling]

    barrier = pltpu.get_barrier_semaphore()
    for dev in partners:
        pl.semaphore_signal(barrier, inc=1, device_id=dev, device_id_type=MESH)

    own_copies = [
        pltpu.make_async_copy(wg_hbm, wgu.at[0, :, pl.ds(0, ff)], local_sem.at[0]),
        pltpu.make_async_copy(wu_hbm, wgu.at[0, :, pl.ds(ff, ff)], local_sem.at[1]),
        pltpu.make_async_copy(wd_hbm, wdn.at[0], local_sem.at[2]),
    ]
    for cp in own_copies:
        cp.start()
    pl.semaphore_wait(barrier, len(partners))

    link = Links(send_sem, recv_sem)

    def part(a, slot, qi, h):
        n = wd_hbm.shape[0] // 4 if a == 2 else width // 4
        start, size = qi * n, n
        if h is not None:
            start, size = start + h * (n // 2), n // 2
        start = pl.multiple_of(start, 16)
        if a == 2:
            return wdn.at[slot, pl.ds(start, size), :]
        return wgu.at[slot, pl.ds(start, size), pl.ds(a * ff, ff)]

    def own_part(a, qi, h):
        ref = (wg_hbm, wu_hbm, wd_hbm)[a]
        n = ref.shape[0] // 4
        return ref.at[pl.ds(pl.multiple_of(qi * n + h * (n // 2), 16), n // 2), :]

    zk = {}
    for a in range(3):
        for h in range(2):
            zk[a, h] = link.new()
            link.start(zk[a, h], own_part(a, y, h), part(a, 2, y, h), at_z(2 if h == 0 else -2))
    mk = []
    slots = [(3, 0), (1, 0), (2, 0), (0, 1), (3, 1), (1, 1), (2, 1)]
    targets = [(1, 0), (3, 0), (2, 0), (0, 1), (1, 1), (3, 1), (2, 1)]
    for i, dev in enumerate(peers):
        mk.append(link.new())
        dx, dz = targets[i]
        sx, sz = slots[i]
        link.start(mk[i], table_ref.at[dx * 2 + dz], meta.at[sx * 2 + sz], dev)
    kz, kr, kl = link.new(), link.new(), link.new()
    link.start(kz, tok_ref, x_buf.at[0, pl.ds(rows, rows)], zp)
    link.start(kr, tok_ref, x_buf.at[3, pl.ds(0, rows)], xr)
    link.start(kl, tok_ref, x_buf.at[1, pl.ds(0, rows)], xl)
    ck = []
    for a, ref in enumerate((wg_hbm, wu_hbm, wd_hbm)):
        ck.append(link.new())
        dst = wdn.at[1] if a == 2 else wgu.at[1, :, pl.ds(a * ff, ff)]
        link.start(ck[a], ref, dst, sibling)
    x_buf[0, 0:rows, :] = tok_ref[...]
    meta[0] = table_ref[0]

    kr1, kl1 = link.new(), link.new()
    link.arrived(kz, x_buf.at[0, pl.ds(rows, rows)], zp)
    link.start(kr1, x_buf.at[0, pl.ds(rows, rows)], x_buf.at[3, pl.ds(rows, rows)], xr)
    link.start(kl1, x_buf.at[0, pl.ds(rows, rows)], x_buf.at[1, pl.ds(rows, rows)], xl)
    fr, fl = {}, {}

    def forward(dz, got_l, got_r):
        r = pl.ds(dz * rows, rows)
        fr[dz], fl[dz] = link.new(), link.new()
        link.arrived(got_l, x_buf.at[3, r], xl)
        link.start(fr[dz], x_buf.at[3, r, pl.ds(0, half)], x_buf.at[2, r, pl.ds(0, half)], xr)
        link.arrived(got_r, x_buf.at[1, r], xr)
        link.start(fl[dz], x_buf.at[1, r, pl.ds(half, half)], x_buf.at[2, r, pl.ds(half, half)], xl)

    forward(0, kr, kl)

    up, down = at_y(1), at_y(-1)
    yk = {}

    def spread(a):
        for h in range(2):
            link.arrived(zk[a, h], part(a, 2, y, h), at_z(-2 if h == 0 else 2))
        for h in range(2):
            for d in (1, -1):
                yk[a, h, d] = link.new()
                link.start(yk[a, h, d], part(a, 2, y, h), part(a, 2, y, h), up if d == 1 else down)
        share(a, y)

    share_k = []

    def share(a, qi):
        k = link.new()
        link.start(k, part(a, 2, qi, None), part(a, 3, qi, None), sibling)
        share_k.append((k, a, qi))

    yp, ym, yo = (y + 1) % 4, (y + 3) % 4, (y + 2) % 4
    fk = {}

    def relay(a):
        link.arrived(yk[a, 0, 1], part(a, 2, ym, 0), down)
        fk[a, 0] = link.new()
        link.start(fk[a, 0], part(a, 2, ym, 0), part(a, 2, ym, 0), up)
        link.arrived(yk[a, 1, -1], part(a, 2, yp, 1), up)
        fk[a, 1] = link.new()
        link.start(fk[a, 1], part(a, 2, yp, 1), part(a, 2, yp, 1), down)
        link.arrived(yk[a, 1, 1], part(a, 2, ym, 1), down)
        link.arrived(yk[a, 0, -1], part(a, 2, yp, 0), up)
        share(a, ym)
        share(a, yp)

    def last(a):
        link.arrived(fk[a, 0], part(a, 2, yo, 0), down)
        link.arrived(fk[a, 1], part(a, 2, yo, 1), up)
        share(a, yo)

    def ffn(dx, base):
        xv = x_buf[dx]
        gates = gcol[dx]
        for j in range(2):
            r = jnp.dot(xv, wgu[base + j], preferred_element_type=F32)
            g, u = r[:, :ff], r[:, ff:]
            s = (0.5 * g) * (1.0 + jnp.tanh(0.5 * g))
            hid[:, j * ff : (j + 1) * ff] = (s * u * gates[:, base + j : base + j + 1]).astype(BF16)

    def first_half(dx):
        ffn(dx, 0)
        w = wdn[0:2].reshape(2 * ff, width)
        acc[dx] = jnp.dot(hid[...], w, preferred_element_type=F32)

    def second_half(dx):
        ffn(dx, 2)
        w = wdn[2:4].reshape(2 * ff, width)
        return acc[dx] + jnp.dot(hid[...], w, preferred_element_type=F32)

    for a in range(3):
        spread(a)
    for i in range(7):
        sx, sz = slots[i]
        link.arrived(mk[i], meta.at[sx * 2 + sz], peers[i])
    for dx in range(4):
        for dz in range(2):
            gcol[dx, dz * rows : (dz + 1) * rows, :] = meta[dx * 2 + dz].T[:rows, :]
    for cp in own_copies:
        cp.wait()
    for a in range(3):
        link.arrived(ck[a], wdn.at[1] if a == 2 else wgu.at[1, :, pl.ds(a * ff, ff)], sibling)
    forward(1, kr1, kl1)
    first_half(0)
    relay(0)
    first_half(1)
    relay(1)
    first_half(3)
    relay(2)
    last(0)
    for dz in range(2):
        r = pl.ds(dz * rows, rows)
        link.arrived(fr[dz], x_buf.at[2, r, pl.ds(0, half)], xl)
        link.arrived(fl[dz], x_buf.at[2, r, pl.ds(half, half)], xr)
    first_half(2)
    last(1)
    last(2)

    for k, a, qi in share_k:
        link.arrived(k, part(a, 3, qi, None), sibling)

    low, high = pl.ds(0, half), pl.ds(half, half)
    p2 = second_half(2)
    sendb[2] = p2.astype(BF16)
    hr, hl, gr, gl = {}, {}, {}, {}
    for dz in (1, 0):
        r = pl.ds(dz * rows, rows)
        hr[dz], hl[dz] = link.new(), link.new()
        link.start(hr[dz], sendb.at[2, r, low], half_in.at[0, r], xr)
        link.start(hl[dz], sendb.at[2, r, high], half_in.at[1, r], xl)
    acc[1] = second_half(1)
    acc[3] = second_half(3)
    for dz in (1, 0):
        r, rs = pl.ds(dz * rows, rows), slice(dz * rows, (dz + 1) * rows)
        gr[dz], gl[dz] = link.new(), link.new()
        link.arrived(hr[dz], half_in.at[0, r], xl)
        sendb[1, rs, :half] = (acc[1, rs, :half] + half_in[0, rs].astype(F32)).astype(BF16)
        sendb[1, rs, half:] = acc[1, rs, half:].astype(BF16)
        link.start(gr[dz], sendb.at[1, r], full_in.at[0, r], xr)
        link.arrived(hl[dz], half_in.at[1, r], xr)
        sendb[3, rs, half:] = (acc[3, rs, half:] + half_in[1, rs].astype(F32)).astype(BF16)
        sendb[3, rs, :half] = acc[3, rs, :half].astype(BF16)
        link.start(gl[dz], sendb.at[3, r], full_in.at[1, r], xl)

    taken = flag_ref[0:1, 0:1] == 1
    sel_g[...] = jnp.where(taken, wgu[2, :, :ff], wgu[0, :, :ff])
    sel_u[...] = jnp.where(taken, wgu[2, :, ff:], wgu[0, :, ff:])
    sel_d[...] = jnp.where(taken, wdn[2], wdn[0])
    out_copies = [
        pltpu.make_async_copy(sel_g, sg_hbm, local_sem.at[3]),
        pltpu.make_async_copy(sel_u, su_hbm, local_sem.at[4]),
        pltpu.make_async_copy(sel_d, sd_hbm, local_sem.at[5]),
    ]
    for cp in out_copies:
        cp.start()

    acc[0] = second_half(0)
    kz2 = link.new()
    rz, r0 = pl.ds(rows, rows), pl.ds(0, rows)
    link.arrived(gr[1], full_in.at[0, rz], xl)
    link.arrived(gl[1], full_in.at[1, rz], xr)
    sendb[0, rows:, :] = (acc[0, rows:, :] + full_in[0, rows:].astype(F32) + full_in[1, rows:].astype(F32)).astype(BF16)
    link.start(kz2, sendb.at[0, rz], z_in, zp)
    link.arrived(gr[0], full_in.at[0, r0], xl)
    link.arrived(gl[0], full_in.at[1, r0], xr)
    total = acc[0, :rows, :] + full_in[0, :rows].astype(F32) + full_in[1, :rows].astype(F32)
    link.arrived(kz2, z_in, zp)
    mixed_ref[...] = (total + z_in[...].astype(F32)).astype(BF16)
    link.finish()
    for cp in out_copies:
        cp.wait()


def per_device(tokens, expert_ids, gate_probs, w_gate, w_up, w_down, placement, swap_flags):
    rows, width = tokens.shape
    ff = w_gate.shape[2]
    ex = lax.axis_index("expert")
    zl, x, c = ex // 8, (ex // 2) % 4, ex % 2
    dx, dz, j = jnp.meshgrid(jnp.arange(4), jnp.arange(2), jnp.arange(4), indexing="ij")
    zt = jnp.where(dz == 1, jnp.bitwise_xor(zl, 1), zl)
    zt = jnp.where(j >= 2, jnp.bitwise_xor(zt, 2), zt)
    dev = (zt * 4 + (x + dx) % 4) * 2 + jnp.where(j % 2 == 1, 1 - c, c)
    wanted = placement[dev.reshape(-1)]
    ids = expert_ids.T
    probs = gate_probs.T
    table = jnp.sum(jnp.where(ids[None] == wanted[:, None, None], probs[None], 0.0), axis=1)
    table = table.reshape(8, 4, rows)
    table = jnp.pad(table, ((0, 0), (0, 4), (0, 128 - rows)))
    flag = jnp.broadcast_to(swap_flags[ex], (8, 128))

    vmem = pl.BlockSpec(memory_space=pltpu.VMEM)
    hbm = pl.BlockSpec(memory_space=pl.ANY)
    mixed, sg, su, sd = pl.pallas_call(
        kernel,
        out_shape=(
            jax.ShapeDtypeStruct((rows, width), BF16),
            jax.ShapeDtypeStruct((width, ff), BF16),
            jax.ShapeDtypeStruct((width, ff), BF16),
            jax.ShapeDtypeStruct((ff, width), BF16),
        ),
        in_specs=[vmem, vmem, vmem, hbm, hbm, hbm],
        out_specs=(vmem, hbm, hbm, hbm),
        scratch_shapes=[
            pltpu.VMEM((4, 2 * rows, width), BF16),
            pltpu.VMEM((8, 8, 128), F32),
            pltpu.VMEM((4, 2 * rows, 8), F32),
            pltpu.VMEM((4, width, 2 * ff), BF16),
            pltpu.VMEM((4, ff, width), BF16),
            pltpu.VMEM((2 * rows, 2 * ff), BF16),
            pltpu.VMEM((4, 2 * rows, width), F32),
            pltpu.VMEM((4, 2 * rows, width), BF16),
            pltpu.VMEM((2, 2 * rows, width // 2), BF16),
            pltpu.VMEM((2, 2 * rows, width), BF16),
            pltpu.VMEM((rows, width), BF16),
            pltpu.VMEM((width, ff), BF16),
            pltpu.VMEM((width, ff), BF16),
            pltpu.VMEM((ff, width), BF16),
            pltpu.SemaphoreType.DMA((80,)),
            pltpu.SemaphoreType.DMA((80,)),
            pltpu.SemaphoreType.DMA((6,)),
        ],
        compiler_params=pltpu.CompilerParams(
            collective_id=0, has_side_effects=True, vmem_limit_bytes=48 * 2**20
        ),
    )(tokens, table, flag, w_gate[0], w_up[0], w_down[0])
    return mixed, sg[None], su[None], sd[None]


def solution(mesh):
    in_specs = (
        P(("dp", "expert"), None),
        P(("dp", "expert"), None),
        P(("dp", "expert"), None),
        P("expert", None, None),
        P("expert", None, None),
        P("expert", None, None),
        P(),
        P(),
    )
    out_specs = (
        P(("dp", "expert"), None),
        P(("dp", "expert"), None, None),
        P(("dp", "expert"), None, None),
        P(("dp", "expert"), None, None),
    )
    return jax.shard_map(
        per_device, mesh=mesh, in_specs=in_specs, out_specs=out_specs, check_vma=False
    )
```

```python
import jax
import jax.numpy as jnp
from jax import lax
from jax.experimental import pallas as pl
from jax.experimental.pallas import tpu as pltpu
from jax.sharding import PartitionSpec as P

MESH = pl.DeviceIdType.MESH
F32 = jnp.float32
BF16 = jnp.bfloat16


class Links:
    def __init__(self, send, recv):
        self.send, self.recv, self.count, self.started = send, recv, 0, []

    def new(self):
        self.count += 1
        return self.count - 1

    def copy(self, k, src, dst, dev):
        return pltpu.make_async_remote_copy(
            src_ref=src,
            dst_ref=dst,
            send_sem=self.send.at[k],
            recv_sem=self.recv.at[k],
            device_id=dev,
            device_id_type=MESH,
        )

    def start(self, k, src, dst, dev):
        c = self.copy(k, src, dst, dev)
        c.start()
        self.started.append(c)

    def arrived(self, k, dst, dev):
        self.copy(k, dst, dst, dev).wait_recv()

    def finish(self):
        for c in self.started:
            c.wait_send()


def kernel(
    ids_ref, prob_ref, flag_ref, place_ref, tok_hbm, wg_hbm, wu_hbm, wd_hbm,
    mixed_ref, sg_ref, su_ref, sd_ref,
    x_buf, flip, table_ref, meta, gcol, wgu, wdn, hid, acc, sendb, half_in, full_in, z_in,
    send_sem, recv_sem, local_sem,
):
    rows, width = tok_hbm.shape
    ff = wg_hbm.shape[1]
    half = width // 2
    dp = lax.axis_index("dp")
    ex = lax.axis_index("expert")
    zh, y = dp // 4, dp % 4
    zl, x, c = ex // 8, (ex // 2) % 4, ex % 2
    zo = zl + 1 - 2 * (zl % 2)

    def at(dx, other):
        return {"dp": dp, "expert": ((zo if other else zl) * 4 + (x + dx + 4) % 4) * 2 + c}

    def at_z(d):
        zz = (zh * 4 + zl + d + 16) % 16
        return {"dp": (zz // 4) * 4 + y, "expert": ((zz % 4) * 4 + x) * 2 + c}

    def at_y(d):
        return {"dp": zh * 4 + (y + d + 4) % 4, "expert": ex}

    sibling = {"dp": dp, "expert": ex + 1 - 2 * c}
    xr, xl, zp = at(1, False), at(-1, False), at(0, True)
    peers = [at(1, False), at(-1, False), at(2, False), at(0, True), at(1, True), at(-1, True), at(2, True)]
    partners = peers + [at_z(2), at_z(-2), at_y(1), at_y(-1), sibling]

    barrier = pltpu.get_barrier_semaphore()
    for dev in partners:
        pl.semaphore_signal(barrier, inc=1, device_id=dev, device_id_type=MESH)

    own_copies = [
        pltpu.make_async_copy(wg_hbm, wgu.at[0, :, pl.ds(0, ff)], local_sem.at[0]),
        pltpu.make_async_copy(wu_hbm, wgu.at[0, :, pl.ds(ff, ff)], local_sem.at[1]),
        pltpu.make_async_copy(wd_hbm, wdn.at[0], local_sem.at[2]),
    ]
    own_tokens = pltpu.make_async_copy(tok_hbm, x_buf.at[0, pl.ds(0, rows)], local_sem.at[3])
    own_tokens.start()
    for cp in own_copies:
        cp.start()

    flip[...] = jnp.zeros_like(flip)
    flip[0, :, 0:rows] = ids_ref[...].astype(F32)
    flip[1, :, 0:rows] = prob_ref[...]
    ids_t, prob_t = flip[0], flip[1]
    for dx in range(4):
        for dz in range(2):
            zt = zo if dz else zl
            for j in range(4):
                zj = (zt + 2) % 4 if j >= 2 else zt
                cj = 1 - c if j % 2 else c
                e = place_ref[(zj * 4 + (x + dx) % 4) * 2 + cj].astype(F32)
                hit = jnp.where(ids_t == e, prob_t, 0.0)
                table_ref[dx * 2 + dz, j : j + 1, :] = jnp.sum(hit, axis=0, keepdims=True)
            table_ref[dx * 2 + dz, 4:8, :] = jnp.zeros((4, 128), F32)
    pl.semaphore_wait(barrier, len(partners))

    link = Links(send_sem, recv_sem)

    pieces = [(0, 0, 128), (0, 128, ff - 128), (1, 0, ff), (2, 0, half), (2, half, half // 2), (2, half + half // 2, half // 2)]

    def row_range(i, qi, h):
        n = (wd_hbm.shape[0] if i == 2 else width) // 4
        start, size = qi * n, n
        if h is not None:
            start, size = start + h * (n // 2), n // 2
        return pl.ds(pl.multiple_of(start, 16), size)

    def part(a, slot, qi, h):
        i, c0, cn = pieces[a]
        r = row_range(i, qi, h)
        if i == 2:
            return wdn.at[slot, r, pl.ds(c0, cn)]
        return wgu.at[slot, r, pl.ds(i * ff + c0, cn)]

    def own_part(a, qi, h):
        i, c0, cn = pieces[a]
        return (wg_hbm, wu_hbm, wd_hbm)[i].at[row_range(i, qi, h), pl.ds(c0, cn)]

    yp, ym, yo = (y + 1) % 4, (y + 3) % 4, (y + 2) % 4
    direct = -1

    zk, ok = {}, {}

    def fetch(a):
        for h in range(2):
            zk[a, h] = link.new()
            link.start(zk[a, h], own_part(a, y, h), part(a, 2, y, h), at_z(2 if h == 0 else -2))

    def fetch_opposite(a):
        for h in range(2):
            ok[a, h] = link.new()
            link.start(ok[a, h], own_part(a, yo, h), part(a, 2, yo, h), at_z(2 if h == 0 else -2))

    mk = []
    slots = [(3, 0), (1, 0), (2, 0), (0, 1), (3, 1), (1, 1), (2, 1)]
    targets = [(1, 0), (3, 0), (2, 0), (0, 1), (1, 1), (3, 1), (2, 1)]

    def tables():
        for i, dev in enumerate(peers):
            mk.append(link.new())
            dx, dz = targets[i]
            sx, sz = slots[i]
            link.start(mk[i], table_ref.at[dx * 2 + dz], meta.at[sx * 2 + sz], dev)

    def tables_here():
        for i in range(7):
            sx, sz = slots[i]
            link.arrived(mk[i], meta.at[sx * 2 + sz], peers[i])
        meta[0] = table_ref[0]
        for dx in range(4):
            for dz in range(2):
                gcol[dx, dz * rows : (dz + 1) * rows, :] = meta[dx * 2 + dz].T[:rows, :]

    kz, kr, kl, kf = {}, {}, {}, {}

    def tok(dx, dz, h):
        return x_buf.at[dx, pl.ds(dz * rows, rows), pl.ds(h * half, half)]

    def pair(h):
        kz[h] = link.new()
        link.start(kz[h], tok_hbm.at[:, pl.ds(h * half, half)], tok(0, 1, h), zp)

    def around(dz, h):
        if dz == 1:
            link.arrived(kz[h], tok(0, 1, h), zp)
        src = tok(0, 1, h) if dz else tok_hbm.at[:, pl.ds(h * half, half)]
        kr[dz, h], kl[dz, h] = link.new(), link.new()
        link.start(kr[dz, h], src, tok(3, dz, h), xr)
        link.start(kl[dz, h], src, tok(1, dz, h), xl)

    def forward(dz, h):
        kf[dz, h] = link.new()
        if h == 0:
            link.arrived(kr[dz, 0], tok(3, dz, 0), xl)
            link.start(kf[dz, 0], tok(3, dz, 0), tok(2, dz, 0), xr)
        else:
            link.arrived(kl[dz, 1], tok(1, dz, 1), xr)
            link.start(kf[dz, 1], tok(1, dz, 1), tok(2, dz, 1), xl)

    def near(dx):
        for dz in range(2):
            if dx == 3:
                link.arrived(kr[dz, 1], tok(3, dz, 1), xl)
            else:
                link.arrived(kl[dz, 0], tok(1, dz, 0), xr)

    def far():
        for dz in range(2):
            link.arrived(kf[dz, 0], tok(2, dz, 0), xl)
            link.arrived(kf[dz, 1], tok(2, dz, 1), xr)

    ck = []

    def own_weights():
        for a, ref in enumerate((wg_hbm, wu_hbm, wd_hbm)):
            ck.append(link.new())
            dst = wdn.at[1] if a == 2 else wgu.at[1, :, pl.ds(a * ff, ff)]
            link.start(ck[a], ref, dst, sibling)

    def own_weights_here():
        for cp in own_copies + [own_tokens]:
            cp.wait()
        for a in range(3):
            link.arrived(ck[a], wdn.at[1] if a == 2 else wgu.at[1, :, pl.ds(a * ff, ff)], sibling)

    up, down = at_y(1), at_y(-1)
    yk = {}

    def spread(a):
        for h in range(2):
            link.arrived(zk[a, h], part(a, 2, y, h), at_z(-2 if h == 0 else 2))
        for h in range(2):
            for d in (1, -1):
                yk[a, h, d] = link.new()
                link.start(yk[a, h, d], part(a, 2, y, h), part(a, 2, y, h), up if d == 1 else down)
        share(a, y)

    share_k = {}

    def share(a, qi):
        k = link.new()
        link.start(k, part(a, 2, qi, None), part(a, 3, qi, None), sibling)
        share_k.setdefault(a, []).append((k, qi))

    fk = {}

    def relay(a):
        link.arrived(yk[a, 0, 1], part(a, 2, ym, 0), down)
        if a != direct:
            fk[a, 0] = link.new()
            link.start(fk[a, 0], part(a, 2, ym, 0), part(a, 2, ym, 0), up)
        link.arrived(yk[a, 1, -1], part(a, 2, yp, 1), up)
        if a != direct:
            fk[a, 1] = link.new()
            link.start(fk[a, 1], part(a, 2, yp, 1), part(a, 2, yp, 1), down)
        link.arrived(yk[a, 1, 1], part(a, 2, ym, 1), down)
        share(a, ym)
        link.arrived(yk[a, 0, -1], part(a, 2, yp, 0), up)
        share(a, yp)

    def last(a):
        if a == direct:
            link.arrived(ok[a, 0], part(a, 2, yo, 0), at_z(-2))
            link.arrived(ok[a, 1], part(a, 2, yo, 1), at_z(2))
        else:
            link.arrived(fk[a, 0], part(a, 2, yo, 0), down)
            link.arrived(fk[a, 1], part(a, 2, yo, 1), up)
        share(a, yo)

    def shared(a):
        for k, qi in share_k[a]:
            link.arrived(k, part(a, 3, qi, None), sibling)

    def ffn(dx, base, hid):
        xv = x_buf[dx]
        gates = gcol[dx]
        for j in range(2):
            r = jnp.dot(xv, wgu[base + j], preferred_element_type=F32)
            g, u = r[:, :ff], r[:, ff:]
            s = (0.5 * g) * (1.0 + jnp.tanh(0.5 * g))
            hid[:, j * ff : (j + 1) * ff] = (s * u * gates[:, base + j : base + j + 1]).astype(BF16)

    def first_half(dx):
        ffn(dx, 0, hid.at[dx])
        w = wdn[0:2].reshape(2 * ff, width)
        acc[dx] = jnp.dot(hid[dx], w, preferred_element_type=F32)

    def second_half(dx):
        w = wdn[2:4].reshape(2 * ff, width)
        return acc[dx] + jnp.dot(hid[dx], w, preferred_element_type=F32)

    hr, hl, gr, gl = {}, {}, {}, {}
    low, high = pl.ds(0, half), pl.ds(half, half)

    def send_far():
        sendb[2] = second_half(2).astype(BF16)
        for dz in (1, 0):
            r = pl.ds(dz * rows, rows)
            hr[dz], hl[dz] = link.new(), link.new()
            link.start(hr[dz], sendb.at[2, r, low], half_in.at[0, r], xr)
            link.start(hl[dz], sendb.at[2, r, high], half_in.at[1, r], xl)

    def send_near(dz):
        r, rs = pl.ds(dz * rows, rows), slice(dz * rows, (dz + 1) * rows)
        gr[dz], gl[dz] = link.new(), link.new()
        link.arrived(hr[dz], half_in.at[0, r], xl)
        sendb[1, rs, :half] = (acc[1, rs, :half] + half_in[0, rs].astype(F32)).astype(BF16)
        sendb[1, rs, half:] = acc[1, rs, half:].astype(BF16)
        link.start(gr[dz], sendb.at[1, r], full_in.at[0, r], xr)
        link.arrived(hl[dz], half_in.at[1, r], xr)
        sendb[3, rs, half:] = (acc[3, rs, half:] + half_in[1, rs].astype(F32)).astype(BF16)
        sendb[3, rs, :half] = acc[3, rs, :half].astype(BF16)
        link.start(gl[dz], sendb.at[3, r], full_in.at[1, r], xl)

    def total(dz):
        r = pl.ds(dz * rows, rows)
        link.arrived(gr[dz], full_in.at[0, r], xl)
        link.arrived(gl[dz], full_in.at[1, r], xr)
        return acc[0, r] + full_in[0, r].astype(F32) + full_in[1, r].astype(F32)

    tables()
    fetch(0)
    around(0, 0)
    around(0, 1)
    fetch(1)
    fetch(2)
    pair(0)
    pair(1)
    fetch(3)
    fetch(4)
    fetch(5)
    own_weights()
    spread(0)
    forward(0, 0)
    forward(0, 1)
    spread(1)
    relay(0)
    tables_here()
    spread(2)
    last(0)
    relay(1)
    around(1, 0)
    own_weights_here()
    around(1, 1)
    first_half(0)
    last(1)
    spread(3)
    forward(1, 0)
    relay(2)
    spread(4)
    spread(5)
    forward(1, 1)
    relay(3)
    near(1)
    first_half(1)
    last(2)
    relay(4)
    near(3)
    first_half(3)
    relay(5)
    last(3)
    far()
    first_half(2)
    for a in range(3):
        shared(a)
    last(4)
    last(5)
    for dx in (2, 1):
        ffn(dx, 2, hid.at[dx])
    for a in range(3, 6):
        shared(a)
    send_far()
    ffn(3, 2, hid.at[3])
    acc[1] = second_half(1)
    acc[3] = second_half(3)
    send_near(1)
    ffn(0, 2, hid.at[0])
    acc[0] = second_half(0)
    send_near(0)
    taken = flag_ref[ex] == 1
    sg_ref[...] = jnp.where(taken, wgu[2, :, :ff], wgu[0, :, :ff])
    su_ref[...] = jnp.where(taken, wgu[2, :, ff:], wgu[0, :, ff:])
    sd_ref[...] = jnp.where(taken, wdn[2], wdn[0])
    sendb[0, rows:, :] = total(1).astype(BF16)
    fz = link.new()
    link.start(fz, sendb.at[0, pl.ds(rows, rows)], z_in, zp)
    t = total(0)
    link.arrived(fz, z_in, zp)
    mixed_ref[...] = (t + z_in[...].astype(F32)).astype(BF16)
    link.finish()


def finish(a, b, c, d, a_out, b_out, c_out, d_out, sem):
    pairs = ((a, a_out), (b, b_out), (c, c_out), (d, d_out))
    copies = [pltpu.make_async_copy(src, dst, sem.at[i]) for i, (src, dst) in enumerate(pairs)]
    for cp in copies:
        cp.start()
    for cp in copies:
        cp.wait()


def per_device(tokens, expert_ids, gate_probs, w_gate, w_up, w_down, placement, swap_flags):
    rows, width = tokens.shape
    ff = w_gate.shape[2]
    vmem = pl.BlockSpec(memory_space=pltpu.VMEM)
    smem = pl.BlockSpec(memory_space=pltpu.SMEM)
    hbm = pl.BlockSpec(memory_space=pltpu.HBM)
    shapes = (
        jax.ShapeDtypeStruct((rows, width), BF16),
        jax.ShapeDtypeStruct((width, ff), BF16),
        jax.ShapeDtypeStruct((width, ff), BF16),
        jax.ShapeDtypeStruct((ff, width), BF16),
    )
    blocks = (tokens, w_gate[0], w_up[0], w_down[0])
    blocks = tuple(pltpu.with_memory_space_constraint(b, pltpu.HBM) for b in blocks)
    results = pl.pallas_call(
        kernel,
        out_shape=shapes,
        in_specs=[vmem, vmem, smem, smem, hbm, hbm, hbm, hbm],
        out_specs=(vmem,) * 4,
        scratch_shapes=[
            pltpu.VMEM((4, 2 * rows, width), BF16),
            pltpu.VMEM((2, expert_ids.shape[1], 128), F32),
            pltpu.VMEM((8, 8, 128), F32),
            pltpu.VMEM((8, 8, 128), F32),
            pltpu.VMEM((4, 2 * rows, 8), F32),
            pltpu.VMEM((4, width, 2 * ff), BF16),
            pltpu.VMEM((4, ff, width), BF16),
            pltpu.VMEM((4, 2 * rows, 2 * ff), BF16),
            pltpu.VMEM((4, 2 * rows, width), F32),
            pltpu.VMEM((4, 2 * rows, width), BF16),
            pltpu.VMEM((2, 2 * rows, width // 2), BF16),
            pltpu.VMEM((2, 2 * rows, width), BF16),
            pltpu.VMEM((rows, width), BF16),
            pltpu.SemaphoreType.DMA((112,)),
            pltpu.SemaphoreType.DMA((112,)),
            pltpu.SemaphoreType.DMA((6,)),
        ],
        compiler_params=pltpu.CompilerParams(
            collective_id=0, has_side_effects=True, vmem_limit_bytes=48 * 2**20
        ),
    )(expert_ids.T, gate_probs.T, swap_flags, placement, *blocks)
    mixed, sg, su, sd = pl.pallas_call(
        finish,
        out_shape=shapes,
        in_specs=[pl.BlockSpec(memory_space=pl.ANY)] * 4,
        out_specs=[hbm] * 4,
        scratch_shapes=[pltpu.SemaphoreType.DMA((4,))],
        compiler_params=pltpu.CompilerParams(vmem_limit_bytes=2**20),
    )(*results)
    return mixed, sg[None], su[None], sd[None]


def solution(mesh):
    in_specs = (
        P(("dp", "expert"), None),
        P(("dp", "expert"), None),
        P(("dp", "expert"), None),
        P("expert", None, None),
        P("expert", None, None),
        P("expert", None, None),
        P(),
        P(),
    )
    out_specs = (
        P(("dp", "expert"), None),
        P(("dp", "expert"), None, None),
        P(("dp", "expert"), None, None),
        P(("dp", "expert"), None, None),
    )
    return jax.shard_map(
        per_device, mesh=mesh, in_specs=in_specs, out_specs=out_specs, check_vma=False
    )
```

```python
import jax
import jax.numpy as jnp
from jax import lax
from jax.experimental import pallas as pl
from jax.experimental.pallas import tpu as pltpu
from jax.sharding import PartitionSpec as P

MESH = pl.DeviceIdType.MESH
F32 = jnp.float32
BF16 = jnp.bfloat16


class Links:
    def __init__(self, send, recv):
        self.send, self.recv, self.count, self.started = send, recv, 0, []

    def new(self):
        self.count += 1
        return self.count - 1

    def copy(self, k, src, dst, dev):
        return pltpu.make_async_remote_copy(
            src_ref=src,
            dst_ref=dst,
            send_sem=self.send.at[k],
            recv_sem=self.recv.at[k],
            device_id=dev,
            device_id_type=MESH,
        )

    def start(self, k, src, dst, dev):
        c = self.copy(k, src, dst, dev)
        c.start()
        self.started.append(c)

    def arrived(self, k, dst, dev):
        self.copy(k, dst, dst, dev).wait_recv()

    def finish(self):
        for c in self.started:
            c.wait_send()


def kernel(
    ids_ref, prob_ref, flag_ref, place_ref, tok_hbm, wg_hbm, wu_hbm, wd_hbm,
    mixed_ref, sg_ref, su_ref, sd_ref,
    x_buf, flip, table_ref, meta, gcol, wgu, wdn, hid, acc, sendb, half_in, full_in, z_in,
    send_sem, recv_sem, local_sem,
):
    rows, width = tok_hbm.shape
    ff = wg_hbm.shape[1]
    half = width // 2
    dp = lax.axis_index("dp")
    ex = lax.axis_index("expert")
    zh, y = dp // 4, dp % 4
    zl, x, c = ex // 8, (ex // 2) % 4, ex % 2
    zo = zl + 1 - 2 * (zl % 2)

    def at(dx, other):
        return {"dp": dp, "expert": ((zo if other else zl) * 4 + (x + dx + 4) % 4) * 2 + c}

    def at_z(d):
        zz = (zh * 4 + zl + d + 16) % 16
        return {"dp": (zz // 4) * 4 + y, "expert": ((zz % 4) * 4 + x) * 2 + c}

    def at_y(d):
        return {"dp": zh * 4 + (y + d + 4) % 4, "expert": ex}

    sibling = {"dp": dp, "expert": ex + 1 - 2 * c}
    xr, xl, zp = at(1, False), at(-1, False), at(0, True)
    peers = [at(1, False), at(-1, False), at(2, False), at(0, True), at(1, True), at(-1, True), at(2, True)]
    partners = peers + [at_z(2), at_z(-2), at_y(1), at_y(-1), sibling]

    barrier = pltpu.get_barrier_semaphore()
    for dev in partners:
        pl.semaphore_signal(barrier, inc=1, device_id=dev, device_id_type=MESH)

    own_copies = [
        pltpu.make_async_copy(wg_hbm, wgu.at[0, :, pl.ds(0, ff)], local_sem.at[0]),
        pltpu.make_async_copy(wu_hbm, wgu.at[0, :, pl.ds(ff, ff)], local_sem.at[1]),
        pltpu.make_async_copy(wd_hbm, wdn.at[0], local_sem.at[2]),
    ]
    own_tokens = pltpu.make_async_copy(tok_hbm, x_buf.at[0, pl.ds(0, rows)], local_sem.at[3])
    own_tokens.start()
    for cp in own_copies:
        cp.start()

    flip[...] = jnp.zeros_like(flip)
    flip[0, :, 0:rows] = ids_ref[...].astype(F32)
    flip[1, :, 0:rows] = prob_ref[...]
    ids_t, prob_t = flip[0], flip[1]
    for dx in range(4):
        for dz in range(2):
            zt = zo if dz else zl
            for j in range(4):
                zj = (zt + 2) % 4 if j >= 2 else zt
                cj = 1 - c if j % 2 else c
                e = place_ref[(zj * 4 + (x + dx) % 4) * 2 + cj].astype(F32)
                hit = jnp.where(ids_t == e, prob_t, 0.0)
                table_ref[dx * 2 + dz, j : j + 1, :] = jnp.sum(hit, axis=0, keepdims=True)
            table_ref[dx * 2 + dz, 4:8, :] = jnp.zeros((4, 128), F32)
    pl.semaphore_wait(barrier, len(partners))

    link = Links(send_sem, recv_sem)

    pieces = [(0, 0, 128), (0, 128, ff - 128), (1, 0, ff), (2, 0, half), (2, half, half)]

    def row_range(i, qi, h):
        n = (wd_hbm.shape[0] if i == 2 else width) // 4
        start, size = qi * n, n
        if h is not None:
            start, size = start + h * (n // 2), n // 2
        return pl.ds(pl.multiple_of(start, 16), size)

    def part(a, slot, qi, h):
        i, c0, cn = pieces[a]
        r = row_range(i, qi, h)
        if i == 2:
            return wdn.at[slot, r, pl.ds(c0, cn)]
        return wgu.at[slot, r, pl.ds(i * ff + c0, cn)]

    def own_part(a, qi, h):
        i, c0, cn = pieces[a]
        return (wg_hbm, wu_hbm, wd_hbm)[i].at[row_range(i, qi, h), pl.ds(c0, cn)]

    yp, ym, yo = (y + 1) % 4, (y + 3) % 4, (y + 2) % 4
    direct = (3, 4)

    zk, ok = {}, {}

    def fetch(a):
        for h in range(2):
            zk[a, h] = link.new()
            link.start(zk[a, h], own_part(a, y, h), part(a, 2, y, h), at_z(2 if h == 0 else -2))

    def fetch_opposite(a):
        for h in range(2):
            ok[a, h] = link.new()
            link.start(ok[a, h], own_part(a, yo, h), part(a, 2, yo, h), at_z(2 if h == 0 else -2))

    mk = []
    slots = [(3, 0), (1, 0), (2, 0), (0, 1), (3, 1), (1, 1), (2, 1)]
    targets = [(1, 0), (3, 0), (2, 0), (0, 1), (1, 1), (3, 1), (2, 1)]

    def tables():
        for i, dev in enumerate(peers):
            mk.append(link.new())
            dx, dz = targets[i]
            sx, sz = slots[i]
            link.start(mk[i], table_ref.at[dx * 2 + dz], meta.at[sx * 2 + sz], dev)

    def tables_here():
        for i in range(7):
            sx, sz = slots[i]
            link.arrived(mk[i], meta.at[sx * 2 + sz], peers[i])
        meta[0] = table_ref[0]
        for dx in range(4):
            for dz in range(2):
                gcol[dx, dz * rows : (dz + 1) * rows, :] = meta[dx * 2 + dz].T[:rows, :]

    kz, kr, kl, kf = {}, {}, {}, {}

    def tok(dx, dz, h):
        return x_buf.at[dx, pl.ds(dz * rows, rows), pl.ds(h * half, half)]

    def pair(h):
        kz[h] = link.new()
        link.start(kz[h], tok_hbm.at[:, pl.ds(h * half, half)], tok(0, 1, h), zp)

    def around(dz, h):
        if dz == 1:
            link.arrived(kz[h], tok(0, 1, h), zp)
        src = tok(0, 1, h) if dz else tok_hbm.at[:, pl.ds(h * half, half)]
        kr[dz, h], kl[dz, h] = link.new(), link.new()
        link.start(kr[dz, h], src, tok(3, dz, h), xr)
        link.start(kl[dz, h], src, tok(1, dz, h), xl)

    def forward(dz, h):
        kf[dz, h] = link.new()
        if h == 0:
            link.arrived(kr[dz, 0], tok(3, dz, 0), xl)
            link.start(kf[dz, 0], tok(3, dz, 0), tok(2, dz, 0), xr)
        else:
            link.arrived(kl[dz, 1], tok(1, dz, 1), xr)
            link.start(kf[dz, 1], tok(1, dz, 1), tok(2, dz, 1), xl)

    def near(dx):
        for dz in range(2):
            if dx == 3:
                link.arrived(kr[dz, 1], tok(3, dz, 1), xl)
            else:
                link.arrived(kl[dz, 0], tok(1, dz, 0), xr)

    def far():
        for dz in range(2):
            link.arrived(kf[dz, 0], tok(2, dz, 0), xl)
            link.arrived(kf[dz, 1], tok(2, dz, 1), xr)

    ck = []

    def own_weights():
        for a, ref in enumerate((wg_hbm, wu_hbm, wd_hbm)):
            ck.append(link.new())
            dst = wdn.at[1] if a == 2 else wgu.at[1, :, pl.ds(a * ff, ff)]
            link.start(ck[a], ref, dst, sibling)

    def own_weights_here():
        for cp in own_copies + [own_tokens]:
            cp.wait()
        for a in range(3):
            link.arrived(ck[a], wdn.at[1] if a == 2 else wgu.at[1, :, pl.ds(a * ff, ff)], sibling)

    up, down = at_y(1), at_y(-1)
    yk = {}

    def spread(a):
        for h in range(2):
            link.arrived(zk[a, h], part(a, 2, y, h), at_z(-2 if h == 0 else 2))
        for h in range(2):
            for d in (1, -1):
                yk[a, h, d] = link.new()
                link.start(yk[a, h, d], part(a, 2, y, h), part(a, 2, y, h), up if d == 1 else down)
        share(a, y)

    share_k = {}

    def share(a, qi):
        k = link.new()
        link.start(k, part(a, 2, qi, None), part(a, 3, qi, None), sibling)
        share_k.setdefault(a, []).append((k, qi))

    fk = {}

    def relay(a):
        link.arrived(yk[a, 0, 1], part(a, 2, ym, 0), down)
        if a not in direct:
            fk[a, 0] = link.new()
            link.start(fk[a, 0], part(a, 2, ym, 0), part(a, 2, ym, 0), up)
        link.arrived(yk[a, 1, -1], part(a, 2, yp, 1), up)
        if a not in direct:
            fk[a, 1] = link.new()
            link.start(fk[a, 1], part(a, 2, yp, 1), part(a, 2, yp, 1), down)
        link.arrived(yk[a, 1, 1], part(a, 2, ym, 1), down)
        share(a, ym)
        link.arrived(yk[a, 0, -1], part(a, 2, yp, 0), up)
        share(a, yp)

    def last(a):
        if a in direct:
            link.arrived(ok[a, 0], part(a, 2, yo, 0), at_z(-2))
            link.arrived(ok[a, 1], part(a, 2, yo, 1), at_z(2))
        else:
            link.arrived(fk[a, 0], part(a, 2, yo, 0), down)
            link.arrived(fk[a, 1], part(a, 2, yo, 1), up)
        share(a, yo)

    def shared(a):
        for k, qi in share_k[a]:
            link.arrived(k, part(a, 3, qi, None), sibling)

    def ffn(dx, base, hid):
        xv = x_buf[dx]
        gates = gcol[dx]
        for j in range(2):
            r = jnp.dot(xv, wgu[base + j], preferred_element_type=F32)
            g, u = r[:, :ff], r[:, ff:]
            s = (0.5 * g) * (1.0 + jnp.tanh(0.5 * g))
            hid[:, j * ff : (j + 1) * ff] = (s * u * gates[:, base + j : base + j + 1]).astype(BF16)

    def first_half(dx):
        ffn(dx, 0, hid.at[dx])
        w = wdn[0:2].reshape(2 * ff, width)
        acc[dx] = jnp.dot(hid[dx], w, preferred_element_type=F32)

    def second_half(dx, cc):
        cols = pl.ds(cc * half, half)
        w = wdn[2:4, :, cols].reshape(2 * ff, half)
        return acc[dx, :, cols] + jnp.dot(hid[dx], w, preferred_element_type=F32)

    quarter = half // 2
    hr, hl, gr, gl, fz = {}, {}, {}, {}, {}

    def send_far(cc):
        c0 = cc * half
        sendb[2, :, c0 : c0 + half] = second_half(2, cc).astype(BF16)
        hr[cc], hl[cc] = link.new(), link.new()
        link.start(hr[cc], sendb.at[2, :, pl.ds(c0, quarter)], half_in.at[0, cc], xr)
        link.start(hl[cc], sendb.at[2, :, pl.ds(c0 + quarter, quarter)], half_in.at[1, cc], xl)

    def own_sum(dx, cc):
        acc[dx, :, cc * half : (cc + 1) * half] = second_half(dx, cc)

    def send_near(cc, dz):
        c0, c1, c2 = cc * half, cc * half + quarter, (cc + 1) * half
        cols = pl.ds(c0, half)
        if dz == 1:
            link.arrived(hr[cc], half_in.at[0, cc], xl)
            link.arrived(hl[cc], half_in.at[1, cc], xr)
        r, rs = pl.ds(dz * rows, rows), slice(dz * rows, (dz + 1) * rows)
        gr[cc, dz], gl[cc, dz] = link.new(), link.new()
        sendb[1, rs, c0:c1] = (acc[1, rs, c0:c1] + half_in[0, cc, rs].astype(F32)).astype(BF16)
        sendb[1, rs, c1:c2] = acc[1, rs, c1:c2].astype(BF16)
        link.start(gr[cc, dz], sendb.at[1, r, cols], full_in.at[0, r, cols], xr)
        sendb[3, rs, c0:c1] = acc[3, rs, c0:c1].astype(BF16)
        sendb[3, rs, c1:c2] = (acc[3, rs, c1:c2] + half_in[1, cc, rs].astype(F32)).astype(BF16)
        link.start(gl[cc, dz], sendb.at[3, r, cols], full_in.at[1, r, cols], xl)

    def total(cc, dz):
        cols, r = pl.ds(cc * half, half), pl.ds(dz * rows, rows)
        link.arrived(gr[cc, dz], full_in.at[0, r, cols], xl)
        link.arrived(gl[cc, dz], full_in.at[1, r, cols], xr)
        return acc[0, r, cols] + full_in[0, r, cols].astype(F32) + full_in[1, r, cols].astype(F32)

    def send_pair(cc):
        cols, r = pl.ds(cc * half, half), pl.ds(rows, rows)
        sendb[0, rows:, cc * half : (cc + 1) * half] = total(cc, 1).astype(BF16)
        fz[cc] = link.new()
        link.start(fz[cc], sendb.at[0, r, cols], z_in.at[:, cols], zp)

    def final(cc):
        cols = pl.ds(cc * half, half)
        t = total(cc, 0)
        link.arrived(fz[cc], z_in.at[:, cols], zp)
        mixed_ref[:, cc * half : (cc + 1) * half] = (t + z_in[:, cols].astype(F32)).astype(BF16)

    tables()
    fetch(0)
    around(0, 0)
    around(0, 1)
    fetch(1)
    fetch(2)
    pair(0)
    pair(1)
    fetch(3)
    fetch_opposite(3)
    fetch(4)
    fetch_opposite(4)
    own_weights()
    spread(0)
    forward(0, 0)
    forward(0, 1)
    spread(1)
    relay(0)
    tables_here()
    spread(2)
    last(0)
    relay(1)
    around(1, 0)
    own_weights_here()
    around(1, 1)
    first_half(0)
    last(1)
    forward(1, 0)
    spread(3)
    relay(2)
    spread(4)
    forward(1, 1)
    last(3)
    near(1)
    first_half(1)
    last(2)
    near(3)
    first_half(3)
    relay(3)
    last(4)
    far()
    first_half(2)
    for a in range(3):
        shared(a)
    ffn(2, 2, hid.at[2])
    shared(3)
    send_far(0)
    relay(4)
    ffn(1, 2, hid.at[1])
    ffn(3, 2, hid.at[3])
    shared(4)
    send_far(1)
    own_sum(1, 0)
    own_sum(3, 0)
    send_near(0, 1)
    own_sum(1, 1)
    own_sum(3, 1)
    send_near(1, 1)
    send_near(0, 0)
    send_near(1, 0)
    ffn(0, 2, hid.at[0])
    own_sum(0, 0)
    own_sum(0, 1)
    send_pair(0)
    send_pair(1)
    taken = flag_ref[ex] == 1
    sg_ref[...] = jnp.where(taken, wgu[2, :, :ff], wgu[0, :, :ff])
    su_ref[...] = jnp.where(taken, wgu[2, :, ff:], wgu[0, :, ff:])
    sd_ref[...] = jnp.where(taken, wdn[2], wdn[0])
    final(0)
    final(1)
    link.finish()


def finish(a, b, c, d, a_out, b_out, c_out, d_out, sem):
    pairs = ((a, a_out), (b, b_out), (c, c_out), (d, d_out))
    copies = [pltpu.make_async_copy(src, dst, sem.at[i]) for i, (src, dst) in enumerate(pairs)]
    for cp in copies:
        cp.start()
    for cp in copies:
        cp.wait()


def per_device(tokens, expert_ids, gate_probs, w_gate, w_up, w_down, placement, swap_flags):
    rows, width = tokens.shape
    ff = w_gate.shape[2]
    vmem = pl.BlockSpec(memory_space=pltpu.VMEM)
    smem = pl.BlockSpec(memory_space=pltpu.SMEM)
    hbm = pl.BlockSpec(memory_space=pltpu.HBM)
    shapes = (
        jax.ShapeDtypeStruct((rows, width), BF16),
        jax.ShapeDtypeStruct((width, ff), BF16),
        jax.ShapeDtypeStruct((width, ff), BF16),
        jax.ShapeDtypeStruct((ff, width), BF16),
    )
    blocks = (tokens, w_gate[0], w_up[0], w_down[0])
    blocks = tuple(pltpu.with_memory_space_constraint(b, pltpu.HBM) for b in blocks)
    results = pl.pallas_call(
        kernel,
        out_shape=shapes,
        in_specs=[vmem, vmem, smem, smem, hbm, hbm, hbm, hbm],
        out_specs=(vmem,) * 4,
        scratch_shapes=[
            pltpu.VMEM((4, 2 * rows, width), BF16),
            pltpu.VMEM((2, expert_ids.shape[1], 128), F32),
            pltpu.VMEM((8, 8, 128), F32),
            pltpu.VMEM((8, 8, 128), F32),
            pltpu.VMEM((4, 2 * rows, 8), F32),
            pltpu.VMEM((4, width, 2 * ff), BF16),
            pltpu.VMEM((4, ff, width), BF16),
            pltpu.VMEM((4, 2 * rows, 2 * ff), BF16),
            pltpu.VMEM((4, 2 * rows, width), F32),
            pltpu.VMEM((4, 2 * rows, width), BF16),
            pltpu.VMEM((2, 2, 2 * rows, width // 4), BF16),
            pltpu.VMEM((2, 2 * rows, width), BF16),
            pltpu.VMEM((rows, width), BF16),
            pltpu.SemaphoreType.DMA((128,)),
            pltpu.SemaphoreType.DMA((128,)),
            pltpu.SemaphoreType.DMA((6,)),
        ],
        compiler_params=pltpu.CompilerParams(
            collective_id=0, has_side_effects=True, vmem_limit_bytes=48 * 2**20
        ),
    )(expert_ids.T, gate_probs.T, swap_flags, placement, *blocks)
    mixed, sg, su, sd = pl.pallas_call(
        finish,
        out_shape=shapes,
        in_specs=[pl.BlockSpec(memory_space=pl.ANY)] * 4,
        out_specs=[hbm] * 4,
        scratch_shapes=[pltpu.SemaphoreType.DMA((4,))],
        compiler_params=pltpu.CompilerParams(vmem_limit_bytes=2**20),
    )(*results)
    return mixed, sg[None], su[None], sd[None]


def solution(mesh):
    in_specs = (
        P(("dp", "expert"), None),
        P(("dp", "expert"), None),
        P(("dp", "expert"), None),
        P("expert", None, None),
        P("expert", None, None),
        P("expert", None, None),
        P(),
        P(),
    )
    out_specs = (
        P(("dp", "expert"), None),
        P(("dp", "expert"), None, None),
        P(("dp", "expert"), None, None),
        P(("dp", "expert"), None, None),
    )
    return jax.shard_map(
        per_device, mesh=mesh, in_specs=in_specs, out_specs=out_specs, check_vma=False
    )
```

```python
import jax
import jax.numpy as jnp
from jax import lax
from jax.experimental import pallas as pl
from jax.experimental.pallas import tpu as pltpu
from jax.sharding import PartitionSpec as P

MESH = pl.DeviceIdType.MESH
F32 = jnp.float32
BF16 = jnp.bfloat16


class Links:
    def __init__(self, send, recv):
        self.send, self.recv, self.count, self.started = send, recv, 0, []

    def new(self):
        self.count += 1
        return self.count - 1

    def copy(self, k, src, dst, dev):
        return pltpu.make_async_remote_copy(
            src_ref=src,
            dst_ref=dst,
            send_sem=self.send.at[k],
            recv_sem=self.recv.at[k],
            device_id=dev,
            device_id_type=MESH,
        )

    def start(self, k, src, dst, dev):
        c = self.copy(k, src, dst, dev)
        c.start()
        self.started.append(c)

    def arrived(self, k, dst, dev):
        self.copy(k, dst, dst, dev).wait_recv()

    def finish(self):
        for c in self.started:
            c.wait_send()


def kernel(
    ids_hbm, prob_hbm, flag_ref, place_ref, tok_hbm, wg_hbm, wu_hbm, wd_hbm,
    mixed_ref, sg_ref, su_ref, sd_ref,
    x_buf, ids_buf, prob_buf, flip, table_ref, meta, gcol, wgu, wdn, hid, acc, sendb, half_in, full_in, z_in,
    send_sem, recv_sem, local_sem,
):
    rows, width = tok_hbm.shape
    ff = wg_hbm.shape[1]
    half = width // 2
    dp = lax.axis_index("dp")
    ex = lax.axis_index("expert")
    zh, y = dp // 4, dp % 4
    zl, x, c = ex // 8, (ex // 2) % 4, ex % 2
    zo = zl + 1 - 2 * (zl % 2)

    def at(dx, other):
        return {"dp": dp, "expert": ((zo if other else zl) * 4 + (x + dx + 4) % 4) * 2 + c}

    def at_z(d):
        zz = (zh * 4 + zl + d + 16) % 16
        return {"dp": (zz // 4) * 4 + y, "expert": ((zz % 4) * 4 + x) * 2 + c}

    def at_y(d):
        return {"dp": zh * 4 + (y + d + 4) % 4, "expert": ex}

    sibling = {"dp": dp, "expert": ex + 1 - 2 * c}
    xr, xl, zp = at(1, False), at(-1, False), at(0, True)
    peers = [at(1, False), at(-1, False), at(2, False), at(0, True), at(1, True), at(-1, True), at(2, True)]
    partners = peers + [at_z(2), at_z(-2), at_y(1), at_y(-1), sibling]

    routes = [
        pltpu.make_async_copy(ids_hbm, ids_buf, local_sem.at[4]),
        pltpu.make_async_copy(prob_hbm, prob_buf, local_sem.at[5]),
    ]
    for cp in routes:
        cp.start()
    barrier = pltpu.get_barrier_semaphore()
    for dev in partners:
        pl.semaphore_signal(barrier, inc=1, device_id=dev, device_id_type=MESH)

    own_copies = [
        pltpu.make_async_copy(wg_hbm, wgu.at[0, :, pl.ds(0, ff)], local_sem.at[0]),
        pltpu.make_async_copy(wu_hbm, wgu.at[0, :, pl.ds(ff, ff)], local_sem.at[1]),
        pltpu.make_async_copy(wd_hbm, wdn.at[0], local_sem.at[2]),
    ]
    own_tokens = pltpu.make_async_copy(tok_hbm, x_buf.at[0, pl.ds(0, rows)], local_sem.at[3])
    own_tokens.start()
    for cp in own_copies:
        cp.start()

    flip[...] = jnp.zeros_like(flip)
    for cp in routes:
        cp.wait()
    flip[0, :, 0:rows] = ids_buf[...].astype(F32)
    flip[1, :, 0:rows] = prob_buf[...]
    ids_t, prob_t = flip[0], flip[1]
    for dx in range(4):
        for dz in range(2):
            zt = zo if dz else zl
            for j in range(4):
                zj = (zt + 2) % 4 if j >= 2 else zt
                cj = 1 - c if j % 2 else c
                e = place_ref[(zj * 4 + (x + dx) % 4) * 2 + cj].astype(F32)
                hit = jnp.where(ids_t == e, prob_t, 0.0)
                table_ref[dx * 2 + dz, j : j + 1, :] = jnp.sum(hit, axis=0, keepdims=True)
            table_ref[dx * 2 + dz, 4:8, :] = jnp.zeros((4, 128), F32)
    pl.semaphore_wait(barrier, len(partners))

    link = Links(send_sem, recv_sem)

    pieces = [(0, 0, 128), (0, 128, ff - 128), (1, 0, ff), (2, 0, half), (2, half, half)]

    def row_range(i, qi, h):
        n = (wd_hbm.shape[0] if i == 2 else width) // 4
        start, size = qi * n, n
        if h is not None:
            start, size = start + h * (n // 2), n // 2
        return pl.ds(pl.multiple_of(start, 16), size)

    def part(a, slot, qi, h):
        i, c0, cn = pieces[a]
        r = row_range(i, qi, h)
        if i == 2:
            return wdn.at[slot, r, pl.ds(c0, cn)]
        return wgu.at[slot, r, pl.ds(i * ff + c0, cn)]

    def own_part(a, qi, h):
        i, c0, cn = pieces[a]
        return (wg_hbm, wu_hbm, wd_hbm)[i].at[row_range(i, qi, h), pl.ds(c0, cn)]

    yp, ym, yo = (y + 1) % 4, (y + 3) % 4, (y + 2) % 4
    direct = (3, 4)

    zk, ok = {}, {}

    def fetch(a):
        for h in range(2):
            zk[a, h] = link.new()
            link.start(zk[a, h], own_part(a, y, h), part(a, 2, y, h), at_z(2 if h == 0 else -2))

    def fetch_opposite(a):
        for h in range(2):
            ok[a, h] = link.new()
            link.start(ok[a, h], own_part(a, yo, h), part(a, 2, yo, h), at_z(2 if h == 0 else -2))

    mk = []
    slots = [(3, 0), (1, 0), (2, 0), (0, 1), (3, 1), (1, 1), (2, 1)]
    targets = [(1, 0), (3, 0), (2, 0), (0, 1), (1, 1), (3, 1), (2, 1)]

    def tables():
        for i, dev in enumerate(peers):
            mk.append(link.new())
            dx, dz = targets[i]
            sx, sz = slots[i]
            link.start(mk[i], table_ref.at[dx * 2 + dz], meta.at[sx * 2 + sz], dev)

    def tables_here():
        for i in range(7):
            sx, sz = slots[i]
            link.arrived(mk[i], meta.at[sx * 2 + sz], peers[i])
        meta[0] = table_ref[0]
        for dx in range(4):
            for dz in range(2):
                gcol[dx, dz * rows : (dz + 1) * rows, :] = meta[dx * 2 + dz].T[:rows, :]

    kz, kr, kl, kf = {}, {}, {}, {}

    def tok(dx, dz, h):
        return x_buf.at[dx, pl.ds(dz * rows, rows), pl.ds(h * half, half)]

    def pair(h):
        kz[h] = link.new()
        link.start(kz[h], tok_hbm.at[:, pl.ds(h * half, half)], tok(0, 1, h), zp)

    def around(dz, h):
        if dz == 1:
            link.arrived(kz[h], tok(0, 1, h), zp)
        src = tok(0, 1, h) if dz else tok_hbm.at[:, pl.ds(h * half, half)]
        kr[dz, h], kl[dz, h] = link.new(), link.new()
        link.start(kr[dz, h], src, tok(3, dz, h), xr)
        link.start(kl[dz, h], src, tok(1, dz, h), xl)

    def forward(dz, h):
        kf[dz, h] = link.new()
        if h == 0:
            link.arrived(kr[dz, 0], tok(3, dz, 0), xl)
            link.start(kf[dz, 0], tok(3, dz, 0), tok(2, dz, 0), xr)
        else:
            link.arrived(kl[dz, 1], tok(1, dz, 1), xr)
            link.start(kf[dz, 1], tok(1, dz, 1), tok(2, dz, 1), xl)

    def near(dx):
        for dz in range(2):
            if dx == 3:
                link.arrived(kr[dz, 1], tok(3, dz, 1), xl)
            else:
                link.arrived(kl[dz, 0], tok(1, dz, 0), xr)

    def far():
        for dz in range(2):
            link.arrived(kf[dz, 0], tok(2, dz, 0), xl)
            link.arrived(kf[dz, 1], tok(2, dz, 1), xr)

    ck = []

    def own_weights():
        for a, ref in enumerate((wg_hbm, wu_hbm, wd_hbm)):
            ck.append(link.new())
            dst = wdn.at[1] if a == 2 else wgu.at[1, :, pl.ds(a * ff, ff)]
            link.start(ck[a], ref, dst, sibling)

    def own_weights_here():
        for cp in own_copies + [own_tokens]:
            cp.wait()
        for a in range(3):
            link.arrived(ck[a], wdn.at[1] if a == 2 else wgu.at[1, :, pl.ds(a * ff, ff)], sibling)

    up, down = at_y(1), at_y(-1)
    yk = {}

    def spread(a):
        for h in range(2):
            link.arrived(zk[a, h], part(a, 2, y, h), at_z(-2 if h == 0 else 2))
        for h in range(2):
            for d in (1, -1):
                yk[a, h, d] = link.new()
                link.start(yk[a, h, d], part(a, 2, y, h), part(a, 2, y, h), up if d == 1 else down)
        share(a, y)

    share_k = {}

    def share(a, qi):
        k = link.new()
        link.start(k, part(a, 2, qi, None), part(a, 3, qi, None), sibling)
        share_k.setdefault(a, []).append((k, qi))

    fk = {}

    def relay(a):
        link.arrived(yk[a, 0, 1], part(a, 2, ym, 0), down)
        if a not in direct:
            fk[a, 0] = link.new()
            link.start(fk[a, 0], part(a, 2, ym, 0), part(a, 2, ym, 0), up)
        link.arrived(yk[a, 1, -1], part(a, 2, yp, 1), up)
        if a not in direct:
            fk[a, 1] = link.new()
            link.start(fk[a, 1], part(a, 2, yp, 1), part(a, 2, yp, 1), down)
        link.arrived(yk[a, 1, 1], part(a, 2, ym, 1), down)
        share(a, ym)
        link.arrived(yk[a, 0, -1], part(a, 2, yp, 0), up)
        share(a, yp)

    def last(a):
        if a in direct:
            link.arrived(ok[a, 0], part(a, 2, yo, 0), at_z(-2))
            link.arrived(ok[a, 1], part(a, 2, yo, 1), at_z(2))
        else:
            link.arrived(fk[a, 0], part(a, 2, yo, 0), down)
            link.arrived(fk[a, 1], part(a, 2, yo, 1), up)
        share(a, yo)

    def shared(a):
        for k, qi in share_k[a]:
            link.arrived(k, part(a, 3, qi, None), sibling)

    def ffn(dx, base, hid):
        xv = x_buf[dx]
        gates = gcol[dx]
        for j in range(2):
            r = jnp.dot(xv, wgu[base + j], preferred_element_type=F32)
            g, u = r[:, :ff], r[:, ff:]
            s = (0.5 * g) * (1.0 + jnp.tanh(0.5 * g))
            hid[:, j * ff : (j + 1) * ff] = (s * u * gates[:, base + j : base + j + 1]).astype(BF16)

    def first_half(dx):
        ffn(dx, 0, hid.at[dx])
        w = wdn[0:2].reshape(2 * ff, width)
        acc[dx] = jnp.dot(hid[dx], w, preferred_element_type=F32)

    def second_half(dx, cc):
        cols = pl.ds(cc * half, half)
        w = wdn[2:4, :, cols].reshape(2 * ff, half)
        return acc[dx, :, cols] + jnp.dot(hid[dx], w, preferred_element_type=F32)

    quarter = half // 2
    hr, hl, gr, gl, fz = {}, {}, {}, {}, {}

    def send_far(cc):
        c0 = cc * half
        sendb[2, :, c0 : c0 + half] = second_half(2, cc).astype(BF16)
        hr[cc], hl[cc] = link.new(), link.new()
        link.start(hr[cc], sendb.at[2, :, pl.ds(c0, quarter)], half_in.at[0, cc], xr)
        link.start(hl[cc], sendb.at[2, :, pl.ds(c0 + quarter, quarter)], half_in.at[1, cc], xl)

    def own_sum(dx, cc):
        acc[dx, :, cc * half : (cc + 1) * half] = second_half(dx, cc)

    def send_near(cc, dz):
        c0, c1, c2 = cc * half, cc * half + quarter, (cc + 1) * half
        cols = pl.ds(c0, half)
        if dz == 1:
            link.arrived(hr[cc], half_in.at[0, cc], xl)
            link.arrived(hl[cc], half_in.at[1, cc], xr)
        r, rs = pl.ds(dz * rows, rows), slice(dz * rows, (dz + 1) * rows)
        gr[cc, dz], gl[cc, dz] = link.new(), link.new()
        sendb[1, rs, c0:c1] = (acc[1, rs, c0:c1] + half_in[0, cc, rs].astype(F32)).astype(BF16)
        sendb[1, rs, c1:c2] = acc[1, rs, c1:c2].astype(BF16)
        link.start(gr[cc, dz], sendb.at[1, r, cols], full_in.at[0, r, cols], xr)
        sendb[3, rs, c0:c1] = acc[3, rs, c0:c1].astype(BF16)
        sendb[3, rs, c1:c2] = (acc[3, rs, c1:c2] + half_in[1, cc, rs].astype(F32)).astype(BF16)
        link.start(gl[cc, dz], sendb.at[3, r, cols], full_in.at[1, r, cols], xl)

    def total(cc, dz):
        cols, r = pl.ds(cc * half, half), pl.ds(dz * rows, rows)
        link.arrived(gr[cc, dz], full_in.at[0, r, cols], xl)
        link.arrived(gl[cc, dz], full_in.at[1, r, cols], xr)
        return acc[0, r, cols] + full_in[0, r, cols].astype(F32) + full_in[1, r, cols].astype(F32)

    def send_pair(cc):
        cols, r = pl.ds(cc * half, half), pl.ds(rows, rows)
        sendb[0, rows:, cc * half : (cc + 1) * half] = total(cc, 1).astype(BF16)
        fz[cc] = link.new()
        link.start(fz[cc], sendb.at[0, r, cols], z_in.at[:, cols], zp)

    def final(cc):
        cols = pl.ds(cc * half, half)
        t = total(cc, 0)
        link.arrived(fz[cc], z_in.at[:, cols], zp)
        mixed_ref[:, cc * half : (cc + 1) * half] = (t + z_in[:, cols].astype(F32)).astype(BF16)

    tables()
    fetch(0)
    around(0, 0)
    around(0, 1)
    fetch(1)
    fetch(2)
    pair(0)
    pair(1)
    fetch(3)
    fetch(4)
    fetch_opposite(3)
    fetch_opposite(4)
    own_weights()
    spread(0)
    forward(0, 0)
    forward(0, 1)
    spread(1)
    relay(0)
    tables_here()
    spread(2)
    last(0)
    relay(1)
    around(1, 0)
    own_weights_here()
    around(1, 1)
    first_half(0)
    last(1)
    forward(1, 0)
    spread(3)
    relay(2)
    spread(4)
    forward(1, 1)
    last(3)
    near(1)
    first_half(1)
    last(2)
    near(3)
    first_half(3)
    relay(3)
    last(4)
    far()
    first_half(2)
    for a in range(3):
        shared(a)
    ffn(2, 2, hid.at[2])
    shared(3)
    send_far(0)
    relay(4)
    ffn(1, 2, hid.at[1])
    ffn(3, 2, hid.at[3])
    shared(4)
    send_far(1)
    own_sum(1, 0)
    own_sum(3, 0)
    send_near(0, 1)
    own_sum(1, 1)
    own_sum(3, 1)
    send_near(1, 1)
    send_near(0, 0)
    send_near(1, 0)
    ffn(0, 2, hid.at[0])
    own_sum(0, 0)
    own_sum(0, 1)
    send_pair(0)
    send_pair(1)
    taken = flag_ref[ex] == 1
    sg_ref[...] = jnp.where(taken, wgu[2, :, :ff], wgu[0, :, :ff])
    su_ref[...] = jnp.where(taken, wgu[2, :, ff:], wgu[0, :, ff:])
    sd_ref[...] = jnp.where(taken, wdn[2], wdn[0])
    final(0)
    final(1)
    link.finish()


def finish(a, b, c, d, a_out, b_out, c_out, d_out, sem):
    pairs = ((a, a_out), (b, b_out), (c, c_out), (d, d_out))
    copies = [pltpu.make_async_copy(src, dst, sem.at[i]) for i, (src, dst) in enumerate(pairs)]
    for cp in copies:
        cp.start()
    for cp in copies:
        cp.wait()


def per_device(tokens, expert_ids, gate_probs, w_gate, w_up, w_down, placement, swap_flags):
    rows, width = tokens.shape
    ff = w_gate.shape[2]
    vmem = pl.BlockSpec(memory_space=pltpu.VMEM)
    smem = pl.BlockSpec(memory_space=pltpu.SMEM)
    hbm = pl.BlockSpec(memory_space=pltpu.HBM)
    shapes = (
        jax.ShapeDtypeStruct((rows, width), BF16),
        jax.ShapeDtypeStruct((width, ff), BF16),
        jax.ShapeDtypeStruct((width, ff), BF16),
        jax.ShapeDtypeStruct((ff, width), BF16),
    )
    blocks = (expert_ids.T, gate_probs.T, swap_flags, placement, tokens, w_gate[0], w_up[0], w_down[0])
    ids, probs, flags, places, *blocks = (pltpu.with_memory_space_constraint(b, pltpu.HBM) for b in blocks)
    results = pl.pallas_call(
        kernel,
        out_shape=shapes,
        in_specs=[hbm, hbm, smem, smem, hbm, hbm, hbm, hbm],
        out_specs=(vmem,) * 4,
        scratch_shapes=[
            pltpu.VMEM((4, 2 * rows, width), BF16),
            pltpu.VMEM(expert_ids.shape[::-1], jnp.int32),
            pltpu.VMEM(expert_ids.shape[::-1], F32),
            pltpu.VMEM((2, expert_ids.shape[1], 128), F32),
            pltpu.VMEM((8, 8, 128), F32),
            pltpu.VMEM((8, 8, 128), F32),
            pltpu.VMEM((4, 2 * rows, 8), F32),
            pltpu.VMEM((4, width, 2 * ff), BF16),
            pltpu.VMEM((4, ff, width), BF16),
            pltpu.VMEM((4, 2 * rows, 2 * ff), BF16),
            pltpu.VMEM((4, 2 * rows, width), F32),
            pltpu.VMEM((4, 2 * rows, width), BF16),
            pltpu.VMEM((2, 2, 2 * rows, width // 4), BF16),
            pltpu.VMEM((2, 2 * rows, width), BF16),
            pltpu.VMEM((rows, width), BF16),
            pltpu.SemaphoreType.DMA((128,)),
            pltpu.SemaphoreType.DMA((128,)),
            pltpu.SemaphoreType.DMA((6,)),
        ],
        compiler_params=pltpu.CompilerParams(
            collective_id=0, has_side_effects=True, vmem_limit_bytes=48 * 2**20
        ),
    )(ids, probs, flags, places, *blocks)
    mixed, sg, su, sd = pl.pallas_call(
        finish,
        out_shape=shapes,
        in_specs=[pl.BlockSpec(memory_space=pl.ANY)] * 4,
        out_specs=[hbm] * 4,
        scratch_shapes=[pltpu.SemaphoreType.DMA((4,))],
        compiler_params=pltpu.CompilerParams(vmem_limit_bytes=2**20),
    )(*results)
    return mixed, sg[None], su[None], sd[None]


def solution(mesh):
    in_specs = (
        P(("dp", "expert"), None),
        P(("dp", "expert"), None),
        P(("dp", "expert"), None),
        P("expert", None, None),
        P("expert", None, None),
        P("expert", None, None),
        P(),
        P(),
    )
    out_specs = (
        P(("dp", "expert"), None),
        P(("dp", "expert"), None, None),
        P(("dp", "expert"), None, None),
        P(("dp", "expert"), None, None),
    )
    return jax.shard_map(
        per_device, mesh=mesh, in_specs=in_specs, out_specs=out_specs, check_vma=False
    )
```

```python
import jax
import jax.numpy as jnp
from jax import lax
from jax.experimental import pallas as pl
from jax.experimental.pallas import tpu as pltpu
from jax.sharding import PartitionSpec as P

MESH = pl.DeviceIdType.MESH
F32 = jnp.float32
BF16 = jnp.bfloat16


class Links:
    def __init__(self, send, recv):
        self.send, self.recv, self.count, self.started = send, recv, 0, []

    def new(self):
        self.count += 1
        return self.count - 1

    def copy(self, k, src, dst, dev):
        return pltpu.make_async_remote_copy(
            src_ref=src,
            dst_ref=dst,
            send_sem=self.send.at[k],
            recv_sem=self.recv.at[k],
            device_id=dev,
            device_id_type=MESH,
        )

    def start(self, k, src, dst, dev):
        c = self.copy(k, src, dst, dev)
        c.start()
        self.started.append(c)

    def arrived(self, k, dst, dev):
        self.copy(k, dst, dst, dev).wait_recv()

    def finish(self):
        for c in self.started:
            c.wait_send()


def kernel(
    ids_hbm, prob_hbm, flag_ref, place_ref, tok_hbm, wg_hbm, wu_hbm, wd_hbm,
    mixed_ref, sg_ref, su_ref, sd_ref,
    x_buf, ids_buf, prob_buf, flip, table_ref, meta, gcol, wgu, wdn, hid, acc, sendb, half_in, full_in, z_in,
    send_sem, recv_sem, local_sem,
):
    rows, width = tok_hbm.shape
    ff = wg_hbm.shape[1]
    half = width // 2
    dp = lax.axis_index("dp")
    ex = lax.axis_index("expert")
    zh, y = dp // 4, dp % 4
    zl, x, c = ex // 8, (ex // 2) % 4, ex % 2
    zo = zl + 1 - 2 * (zl % 2)

    def at(dx, other):
        return {"dp": dp, "expert": ((zo if other else zl) * 4 + (x + dx + 4) % 4) * 2 + c}

    def at_z(d):
        zz = (zh * 4 + zl + d + 16) % 16
        return {"dp": (zz // 4) * 4 + y, "expert": ((zz % 4) * 4 + x) * 2 + c}

    def at_y(d):
        return {"dp": zh * 4 + (y + d + 4) % 4, "expert": ex}

    sibling = {"dp": dp, "expert": ex + 1 - 2 * c}
    xr, xl, zp = at(1, False), at(-1, False), at(0, True)
    peers = [at(1, False), at(-1, False), at(2, False), at(0, True), at(1, True), at(-1, True), at(2, True)]
    partners = peers + [at_z(2), at_z(-2), at_y(1), at_y(-1), sibling]

    routes = [
        pltpu.make_async_copy(ids_hbm, ids_buf, local_sem.at[4]),
        pltpu.make_async_copy(prob_hbm, prob_buf, local_sem.at[5]),
    ]
    for cp in routes:
        cp.start()
    barrier = pltpu.get_barrier_semaphore()
    for dev in partners:
        pl.semaphore_signal(barrier, inc=1, device_id=dev, device_id_type=MESH)

    own_copies = [
        pltpu.make_async_copy(wg_hbm, wgu.at[0, :, pl.ds(0, ff)], local_sem.at[0]),
        pltpu.make_async_copy(wu_hbm, wgu.at[0, :, pl.ds(ff, ff)], local_sem.at[1]),
        pltpu.make_async_copy(wd_hbm, wdn.at[0], local_sem.at[2]),
    ]
    own_tokens = pltpu.make_async_copy(tok_hbm, x_buf.at[0, pl.ds(0, rows)], local_sem.at[3])
    own_tokens.start()
    for cp in own_copies:
        cp.start()

    flip[...] = jnp.zeros_like(flip)
    for cp in routes:
        cp.wait()
    flip[0, :, 0:rows] = ids_buf[...].astype(F32)
    flip[1, :, 0:rows] = prob_buf[...]
    ids_t, prob_t = flip[0], flip[1]
    for dx in range(4):
        for dz in range(2):
            zt = zo if dz else zl
            for j in range(4):
                zj = (zt + 2) % 4 if j >= 2 else zt
                cj = 1 - c if j % 2 else c
                e = place_ref[(zj * 4 + (x + dx) % 4) * 2 + cj].astype(F32)
                hit = jnp.where(ids_t == e, prob_t, 0.0)
                table_ref[dx * 2 + dz, j : j + 1, :] = jnp.sum(hit, axis=0, keepdims=True)
            table_ref[dx * 2 + dz, 4:8, :] = jnp.zeros((4, 128), F32)
    pl.semaphore_wait(barrier, len(partners))

    link = Links(send_sem, recv_sem)

    pieces = [(0, 0, 128), (0, 128, ff - 128), (1, 0, ff), (2, 0, half), (2, half, half)]

    def row_range(i, qi, h):
        n = (wd_hbm.shape[0] if i == 2 else width) // 4
        start, size = qi * n, n
        if h is not None:
            start, size = start + h * (n // 2), n // 2
        return pl.ds(pl.multiple_of(start, 16), size)

    def part(a, slot, qi, h):
        i, c0, cn = pieces[a]
        r = row_range(i, qi, h)
        if i == 2:
            return wdn.at[slot, r, pl.ds(c0, cn)]
        return wgu.at[slot, r, pl.ds(i * ff + c0, cn)]

    def own_part(a, qi, h):
        i, c0, cn = pieces[a]
        return (wg_hbm, wu_hbm, wd_hbm)[i].at[row_range(i, qi, h), pl.ds(c0, cn)]

    yp, ym, yo = (y + 1) % 4, (y + 3) % 4, (y + 2) % 4
    direct = (3, 4)

    zk, ok = {}, {}

    def fetch(a):
        for h in range(2):
            zk[a, h] = link.new()
            link.start(zk[a, h], own_part(a, y, h), part(a, 2, y, h), at_z(2 if h == 0 else -2))

    def fetch_opposite(a):
        for h in range(2):
            ok[a, h] = link.new()
            link.start(ok[a, h], own_part(a, yo, h), part(a, 2, yo, h), at_z(2 if h == 0 else -2))

    mk = []
    slots = [(3, 0), (1, 0), (2, 0), (0, 1), (3, 1), (1, 1), (2, 1)]
    targets = [(1, 0), (3, 0), (2, 0), (0, 1), (1, 1), (3, 1), (2, 1)]

    def tables():
        for i, dev in enumerate(peers):
            mk.append(link.new())
            dx, dz = targets[i]
            sx, sz = slots[i]
            link.start(mk[i], table_ref.at[dx * 2 + dz], meta.at[sx * 2 + sz], dev)

    def tables_here():
        for i in range(7):
            sx, sz = slots[i]
            link.arrived(mk[i], meta.at[sx * 2 + sz], peers[i])
        meta[0] = table_ref[0]
        for dx in range(4):
            for dz in range(2):
                gcol[dx, dz * rows : (dz + 1) * rows, :] = meta[dx * 2 + dz].T[:rows, :]

    kz, kr, kl, kf = {}, {}, {}, {}

    def tok(dx, dz, h):
        return x_buf.at[dx, pl.ds(dz * rows, rows), pl.ds(h * half, half)]

    def pair(h):
        kz[h] = link.new()
        link.start(kz[h], tok_hbm.at[:, pl.ds(h * half, half)], tok(0, 1, h), zp)

    def around(dz, h):
        if dz == 1:
            link.arrived(kz[h], tok(0, 1, h), zp)
        src = tok(0, 1, h) if dz else tok_hbm.at[:, pl.ds(h * half, half)]
        kr[dz, h], kl[dz, h] = link.new(), link.new()
        link.start(kr[dz, h], src, tok(3, dz, h), xr)
        link.start(kl[dz, h], src, tok(1, dz, h), xl)

    def forward(dz, h):
        kf[dz, h] = link.new()
        if h == 0:
            link.arrived(kr[dz, 0], tok(3, dz, 0), xl)
            link.start(kf[dz, 0], tok(3, dz, 0), tok(2, dz, 0), xr)
        else:
            link.arrived(kl[dz, 1], tok(1, dz, 1), xr)
            link.start(kf[dz, 1], tok(1, dz, 1), tok(2, dz, 1), xl)

    def near(dx):
        for dz in range(2):
            if dx == 3:
                link.arrived(kr[dz, 1], tok(3, dz, 1), xl)
            else:
                link.arrived(kl[dz, 0], tok(1, dz, 0), xr)

    def far():
        for dz in range(2):
            link.arrived(kf[dz, 0], tok(2, dz, 0), xl)
            link.arrived(kf[dz, 1], tok(2, dz, 1), xr)

    ck = []

    def own_weights():
        for a, ref in enumerate((wg_hbm, wu_hbm, wd_hbm)):
            ck.append(link.new())
            dst = wdn.at[1] if a == 2 else wgu.at[1, :, pl.ds(a * ff, ff)]
            link.start(ck[a], ref, dst, sibling)

    def own_weights_here():
        for cp in own_copies + [own_tokens]:
            cp.wait()
        for a in range(3):
            link.arrived(ck[a], wdn.at[1] if a == 2 else wgu.at[1, :, pl.ds(a * ff, ff)], sibling)

    up, down = at_y(1), at_y(-1)
    yk = {}

    def spread(a):
        for h in range(2):
            link.arrived(zk[a, h], part(a, 2, y, h), at_z(-2 if h == 0 else 2))
        for h in range(2):
            for d in (1, -1):
                yk[a, h, d] = link.new()
                link.start(yk[a, h, d], part(a, 2, y, h), part(a, 2, y, h), up if d == 1 else down)
        share(a, y)

    share_k = {}

    def share(a, qi):
        k = link.new()
        link.start(k, part(a, 2, qi, None), part(a, 3, qi, None), sibling)
        share_k.setdefault(a, []).append((k, qi))

    fk = {}

    def relay(a):
        link.arrived(yk[a, 0, 1], part(a, 2, ym, 0), down)
        if a not in direct:
            fk[a, 0] = link.new()
            link.start(fk[a, 0], part(a, 2, ym, 0), part(a, 2, ym, 0), up)
        link.arrived(yk[a, 1, -1], part(a, 2, yp, 1), up)
        if a not in direct:
            fk[a, 1] = link.new()
            link.start(fk[a, 1], part(a, 2, yp, 1), part(a, 2, yp, 1), down)
        link.arrived(yk[a, 1, 1], part(a, 2, ym, 1), down)
        share(a, ym)
        link.arrived(yk[a, 0, -1], part(a, 2, yp, 0), up)
        share(a, yp)

    def last(a):
        if a in direct:
            link.arrived(ok[a, 0], part(a, 2, yo, 0), at_z(-2))
            link.arrived(ok[a, 1], part(a, 2, yo, 1), at_z(2))
        else:
            link.arrived(fk[a, 0], part(a, 2, yo, 0), down)
            link.arrived(fk[a, 1], part(a, 2, yo, 1), up)
        share(a, yo)

    def shared(a):
        for k, qi in share_k[a]:
            link.arrived(k, part(a, 3, qi, None), sibling)

    def ffn(dx, base, hid):
        xv = x_buf[dx]
        gates = gcol[dx]
        for j in range(2):
            r = jnp.dot(xv, wgu[base + j], preferred_element_type=F32)
            g, u = r[:, :ff], r[:, ff:]
            s = (0.5 * g) * (1.0 + jnp.tanh(0.5 * g))
            hid[:, j * ff : (j + 1) * ff] = (s * u * gates[:, base + j : base + j + 1]).astype(BF16)

    def first_half(dx):
        ffn(dx, 0, hid.at[dx])
        w = wdn[0:2].reshape(2 * ff, width)
        acc[dx] = jnp.dot(hid[dx], w, preferred_element_type=F32)

    def second_half(dx, cc):
        cols = pl.ds(cc * half, half)
        w = wdn[2:4, :, cols].reshape(2 * ff, half)
        return acc[dx, :, cols] + jnp.dot(hid[dx], w, preferred_element_type=F32)

    quarter = half // 2
    hr, hl, gr, gl, fz = {}, {}, {}, {}, {}

    def send_far(cc):
        c0 = cc * half
        sendb[2, :, c0 : c0 + half] = second_half(2, cc).astype(BF16)
        hr[cc], hl[cc] = link.new(), link.new()
        link.start(hr[cc], sendb.at[2, :, pl.ds(c0, quarter)], half_in.at[0, cc], xr)
        link.start(hl[cc], sendb.at[2, :, pl.ds(c0 + quarter, quarter)], half_in.at[1, cc], xl)

    def own_sum(dx, cc):
        acc[dx, :, cc * half : (cc + 1) * half] = second_half(dx, cc)

    def send_near(cc, dz):
        c0, c1, c2 = cc * half, cc * half + quarter, (cc + 1) * half
        cols = pl.ds(c0, half)
        if dz == 1:
            link.arrived(hr[cc], half_in.at[0, cc], xl)
            link.arrived(hl[cc], half_in.at[1, cc], xr)
        r, rs = pl.ds(dz * rows, rows), slice(dz * rows, (dz + 1) * rows)
        gr[cc, dz], gl[cc, dz] = link.new(), link.new()
        sendb[1, rs, c0:c1] = (acc[1, rs, c0:c1] + half_in[0, cc, rs].astype(F32)).astype(BF16)
        sendb[1, rs, c1:c2] = acc[1, rs, c1:c2].astype(BF16)
        link.start(gr[cc, dz], sendb.at[1, r, cols], full_in.at[0, r, cols], xr)
        sendb[3, rs, c0:c1] = acc[3, rs, c0:c1].astype(BF16)
        sendb[3, rs, c1:c2] = (acc[3, rs, c1:c2] + half_in[1, cc, rs].astype(F32)).astype(BF16)
        link.start(gl[cc, dz], sendb.at[3, r, cols], full_in.at[1, r, cols], xl)

    def total(cc, dz):
        cols, r = pl.ds(cc * half, half), pl.ds(dz * rows, rows)
        link.arrived(gr[cc, dz], full_in.at[0, r, cols], xl)
        link.arrived(gl[cc, dz], full_in.at[1, r, cols], xr)
        return acc[0, r, cols] + full_in[0, r, cols].astype(F32) + full_in[1, r, cols].astype(F32)

    def send_pair(cc):
        cols, r = pl.ds(cc * half, half), pl.ds(rows, rows)
        sendb[0, rows:, cc * half : (cc + 1) * half] = total(cc, 1).astype(BF16)
        fz[cc] = link.new()
        link.start(fz[cc], sendb.at[0, r, cols], z_in.at[:, cols], zp)

    def final(cc):
        cols = pl.ds(cc * half, half)
        t = total(cc, 0)
        link.arrived(fz[cc], z_in.at[:, cols], zp)
        mixed_ref[:, cc * half : (cc + 1) * half] = (t + z_in[:, cols].astype(F32)).astype(BF16)

    tables()
    fetch(0)
    around(0, 0)
    around(0, 1)
    fetch(1)
    fetch(2)
    pair(0)
    pair(1)
    fetch(3)
    fetch(4)
    fetch_opposite(3)
    fetch_opposite(4)
    own_weights()
    spread(0)
    forward(0, 0)
    forward(0, 1)
    spread(1)
    relay(0)
    tables_here()
    spread(2)
    last(0)
    relay(1)
    around(1, 0)
    own_weights_here()
    around(1, 1)
    first_half(0)
    last(1)
    forward(1, 0)
    spread(3)
    relay(2)
    spread(4)
    forward(1, 1)
    last(3)
    near(1)
    first_half(1)
    last(2)
    near(3)
    relay(3)
    last(4)
    far()
    first_half(2)
    for a in range(3):
        shared(a)
    ffn(2, 2, hid.at[2])
    shared(3)
    send_far(0)
    relay(4)
    ffn(1, 2, hid.at[1])
    first_half(3)
    ffn(3, 2, hid.at[3])
    shared(4)
    send_far(1)
    own_sum(1, 0)
    own_sum(3, 0)
    send_near(0, 1)
    own_sum(1, 1)
    own_sum(3, 1)
    send_near(1, 1)
    send_near(0, 0)
    send_near(1, 0)
    ffn(0, 2, hid.at[0])
    own_sum(0, 0)
    own_sum(0, 1)
    send_pair(0)
    send_pair(1)
    taken = flag_ref[ex] == 1
    sg_ref[...] = jnp.where(taken, wgu[2, :, :ff], wgu[0, :, :ff])
    su_ref[...] = jnp.where(taken, wgu[2, :, ff:], wgu[0, :, ff:])
    sd_ref[...] = jnp.where(taken, wdn[2], wdn[0])
    final(0)
    final(1)
    link.finish()


def finish(a, b, c, d, a_out, b_out, c_out, d_out, sem):
    pairs = ((a, a_out), (b, b_out), (c, c_out), (d, d_out))
    copies = [pltpu.make_async_copy(src, dst, sem.at[i]) for i, (src, dst) in enumerate(pairs)]
    for cp in copies:
        cp.start()
    for cp in copies:
        cp.wait()


def per_device(tokens, expert_ids, gate_probs, w_gate, w_up, w_down, placement, swap_flags):
    rows, width = tokens.shape
    ff = w_gate.shape[2]
    vmem = pl.BlockSpec(memory_space=pltpu.VMEM)
    smem = pl.BlockSpec(memory_space=pltpu.SMEM)
    hbm = pl.BlockSpec(memory_space=pltpu.HBM)
    shapes = (
        jax.ShapeDtypeStruct((rows, width), BF16),
        jax.ShapeDtypeStruct((width, ff), BF16),
        jax.ShapeDtypeStruct((width, ff), BF16),
        jax.ShapeDtypeStruct((ff, width), BF16),
    )
    blocks = (expert_ids.T, gate_probs.T, swap_flags, placement, tokens, w_gate[0], w_up[0], w_down[0])
    ids, probs, flags, places, *blocks = (pltpu.with_memory_space_constraint(b, pltpu.HBM) for b in blocks)
    results = pl.pallas_call(
        kernel,
        out_shape=shapes,
        in_specs=[hbm, hbm, smem, smem, hbm, hbm, hbm, hbm],
        out_specs=(vmem,) * 4,
        scratch_shapes=[
            pltpu.VMEM((4, 2 * rows, width), BF16),
            pltpu.VMEM(expert_ids.shape[::-1], jnp.int32),
            pltpu.VMEM(expert_ids.shape[::-1], F32),
            pltpu.VMEM((2, expert_ids.shape[1], 128), F32),
            pltpu.VMEM((8, 8, 128), F32),
            pltpu.VMEM((8, 8, 128), F32),
            pltpu.VMEM((4, 2 * rows, 8), F32),
            pltpu.VMEM((4, width, 2 * ff), BF16),
            pltpu.VMEM((4, ff, width), BF16),
            pltpu.VMEM((4, 2 * rows, 2 * ff), BF16),
            pltpu.VMEM((4, 2 * rows, width), F32),
            pltpu.VMEM((4, 2 * rows, width), BF16),
            pltpu.VMEM((2, 2, 2 * rows, width // 4), BF16),
            pltpu.VMEM((2, 2 * rows, width), BF16),
            pltpu.VMEM((rows, width), BF16),
            pltpu.SemaphoreType.DMA((128,)),
            pltpu.SemaphoreType.DMA((128,)),
            pltpu.SemaphoreType.DMA((6,)),
        ],
        compiler_params=pltpu.CompilerParams(
            collective_id=0, has_side_effects=True, vmem_limit_bytes=48 * 2**20
        ),
    )(ids, probs, flags, places, *blocks)
    mixed, sg, su, sd = pl.pallas_call(
        finish,
        out_shape=shapes,
        in_specs=[pl.BlockSpec(memory_space=pl.ANY)] * 4,
        out_specs=[hbm] * 4,
        scratch_shapes=[pltpu.SemaphoreType.DMA((4,))],
        compiler_params=pltpu.CompilerParams(vmem_limit_bytes=2**20),
    )(*results)
    return mixed, sg[None], su[None], sd[None]


def solution(mesh):
    in_specs = (
        P(("dp", "expert"), None),
        P(("dp", "expert"), None),
        P(("dp", "expert"), None),
        P("expert", None, None),
        P("expert", None, None),
        P("expert", None, None),
        P(),
        P(),
    )
    out_specs = (
        P(("dp", "expert"), None),
        P(("dp", "expert"), None, None),
        P(("dp", "expert"), None, None),
        P(("dp", "expert"), None, None),
    )
    return jax.shard_map(
        per_device, mesh=mesh, in_specs=in_specs, out_specs=out_specs, check_vma=False
    )
```
